32 devices in a mesh: dp: 4 (over x, core), ctx: 8 (over z, y).
Axes of the slice: x: 2, y: 2, z: 4, core: 2. Of those that a mesh axis runs over, the one named last changes fastest.
Arguments:
- out_grad: bfloat16 [16384, 4608], P(('dp', 'ctx')), may hold values from -1 to 1
- adapter_inner: bfloat16 [16384, 16], P(('dp', 'ctx')), may hold values from -32 to 32
- doc_lengths: int32 [4, 4], P('dp'), may hold values from 1 to 1536, 4096 in all within a row
- slab_offset: int32 [4], P('dp'), may hold values from 1 to 1535
- included: int32 [4, 4], P('dp'), may hold values 0 or 1
Outputs:
- adapter_second_gradient: float32 [4608, 16], P(('dp', 'ctx'))
- doc_norms: float32 [4, 4], P('dp')
The draws below stay inside these ranges and needn't reach their ends.
Inputs may be any that keep to these rules, and one draw needn't show every extreme that they name: `doc_lengths`: in each row the lengths sum to 4096, and the largest is exactly 1536.
All inputs are finite; a program needn't handle non-finite values. No bound on the sum of `included` on one device may be relied on, other than what follows from the above.
Results may differ from the reference program's by a relative error of at most 0.0022.
Values may be sent and summed in bfloat16 or wider, within the bound.
No kernel may reach another device: no remote copies, remote signals or barrier semaphores. Data moves between devices by JAX's collectives and lax.ppermute only.
A program may use at most 64 MiB of HBM per device.

```python
import math
import jax
import jax.numpy as jnp
import numpy as np
from jax import lax

D = 4608
RANK = 16
CB = 512
LMAX = 1536
BATCHES = 4
NDOC = 4
TOKB = 4096
TOKENS = 16384
N_CTX = 8


def common_part(key, row_count, col_count):
    anchor_count = row_count // CB + 1
    anchors = jax.random.normal(key, (anchor_count, col_count), jnp.float32)
    positions = jnp.arange(row_count)
    lower_node = positions // CB
    fraction = (positions % CB).astype(jnp.float32) / CB
    return anchors[lower_node] * (1.0 - fraction)[:, None] + anchors[lower_node + 1] * fraction[:, None]


def noisy_rows(key, row_count, col_count):
    subkeys = jax.random.split(key, 2)
    noise_part = jax.random.truncated_normal(subkeys[0], -4.0, 4.0, (row_count, col_count), jnp.float32)
    common = common_part(subkeys[1], row_count, col_count)
    return noise_part + CB ** (-0.25) * common


def draw_adapter_inner(key, part):
    values = noisy_rows(jax.random.fold_in(key, 11), TOKENS, RANK)
    return jnp.clip(values, -32.0, 32.0).astype(jnp.bfloat16)


def draw_out_grad(key, part):
    values = noisy_rows(jax.random.fold_in(key, 23), TOKENS, D) * D ** (-0.5)
    return jnp.clip(values, -1.0, 1.0).astype(jnp.bfloat16)


def with_ends(values, key, low, top_value):
    longest = values.shape.index(max(values.shape))
    spots = []
    for shift in (0, 1):
        where = [jax.random.randint(jax.random.fold_in(key, axis), (), 0, length) for axis, length in enumerate(values.shape)]
        where[longest] = (where[longest] + shift) % values.shape[longest]
        spots.append(tuple(where))
    return values.at[spots[0]].set(low).at[spots[1]].set(top_value)


def profile(amount, total, bound, skew):
    portions = [(1 << 20) // math.isqrt(standing ** skew) + 1 for standing in range(2, amount + 1)]
    rest, given = total - bound - (amount - 1), [1] * (amount - 1)
    while rest > 0:
        candidates = [i for i in range(amount - 1) if given[i] < bound]
        mass, remaining = sum([portions[i] for i in candidates]), rest
        for i in candidates:
            more = min(bound - given[i], max(1, remaining * portions[i] // mass), rest)
            given[i] = given[i] + more
            rest = rest - more
    return np.array([bound] + given)


def uneven_parts(own_key, number_of, total, bound, slope):
    if number_of == 2:
        one = jax.random.randint(own_key, (), max(1, total - bound), min(bound, total - 1) + 1)
        return jnp.stack([one, total - one])
    sizes = jnp.asarray(profile(number_of, total, bound, slope), jnp.int32)
    couples = (number_of - 1) // 2
    donor, sink = sizes[1:1 + 2 * couples:2], sizes[2:2 + 2 * couples:2]
    slack = jnp.minimum(donor - 1, bound - sink)
    moved = jax.random.randint(jax.random.fold_in(own_key, 1), (couples,), 0, 1 << 20) % (slack + 1)
    sizes = sizes.at[1:1 + 2 * couples:2].set(donor - moved).at[2:2 + 2 * couples:2].set(sink + moved)
    return sizes[jax.random.permutation(jax.random.fold_in(own_key, 2), number_of)]


def setup_inputs(seed: int = 0) -> dict:
    keys = jax.random.split(jax.random.key(seed), 6)
    out_grad = draw_out_grad(jax.random.fold_in(keys[5], 71), 0)
    adapter_inner = draw_adapter_inner(jax.random.fold_in(keys[5], 71), 0)
    doc_lengths = jax.vmap(lambda own: uneven_parts(own, NDOC, TOKB, LMAX, 1))(jax.random.split(keys[2], BATCHES)).reshape((BATCHES, NDOC)).astype(jnp.int32)
    slab_offset = with_ends(jax.random.randint(keys[3], (BATCHES,), 1, LMAX), jax.random.fold_in(keys[3], 1), 1, LMAX - 1).astype(jnp.int32)
    included = with_ends((jax.random.randint(keys[4], (BATCHES, NDOC), 0, 2) < 1).astype(jnp.int32), jax.random.fold_in(keys[4], 1), 0, 1)
    return dict(out_grad=out_grad, adapter_inner=adapter_inner, doc_lengths=doc_lengths, slab_offset=slab_offset, included=included)


clip_norm = 128.0

def document_ids(lengths, offset, positions):
    doc_ends = jnp.cumsum(lengths).astype(jnp.int32)
    starts = (doc_ends - lengths).astype(jnp.int32)
    longest = jnp.argmax(lengths).astype(jnp.int32)
    labels = jnp.arange(lengths.shape[0], dtype=jnp.int32)
    doc_shift = jnp.sum(jnp.where(labels == longest, starts, 0)).astype(jnp.int32) + offset
    packed = (positions + doc_shift) % (N_CTX * CB)
    return lax.optimization_barrier(jnp.sum((doc_ends[None, :] <= packed[:, None]).astype(jnp.int32), axis=1)).astype(jnp.int32)

def per_document(inner_rows, grad_rows, doc_ids):
    inner_blocks = inner_rows.reshape(N_CTX, CB, RANK)
    grad_blocks = grad_rows.reshape(N_CTX, CB, D)
    id_blocks = doc_ids.reshape(N_CTX, CB)
    labels = jnp.arange(NDOC, dtype=jnp.int32)

    def add_block(accumulated, block_items):
        inner_block, grad_block, id_block = block_items
        member = (id_block[:, None] == labels[None, :]).astype(jnp.float32)
        spread = (member[:, :, None] * inner_block.astype(jnp.float32)[:, None, :]).reshape(CB, NDOC * RANK)
        return (accumulated + jnp.dot(spread.T, grad_block.astype(jnp.float32), precision=lax.Precision.HIGHEST), None)
    result, unused = lax.scan(add_block, jnp.zeros((NDOC * RANK, D), jnp.float32), (inner_blocks, grad_blocks, id_blocks))
    return result

def reference(out_grad, adapter_inner, doc_lengths, slab_offset, included):
    tokens_batch = N_CTX * CB
    total_grad = jnp.zeros((D, RANK), jnp.float32)
    row_norm_values = []
    for batch_index in range(BATCHES):
        first_row = batch_index * tokens_batch
        inner_rows = adapter_inner[first_row:first_row + tokens_batch]
        grad_rows = out_grad[first_row:first_row + tokens_batch]
        doc_ids = document_ids(doc_lengths[batch_index], slab_offset[batch_index], jnp.arange(tokens_batch, dtype=jnp.int32))
        document_gradient_rows = per_document(inner_rows, grad_rows, doc_ids)
        document_grad_norm = jnp.sqrt(lax.optimization_barrier(jnp.sum(document_gradient_rows.reshape(NDOC, RANK * D) ** 2, axis=1)))
        clip_factor = included[batch_index].astype(jnp.float32) * clip_norm / jnp.maximum(document_grad_norm, clip_norm)
        scaled = (clip_factor[doc_ids][:, None] * inner_rows.astype(jnp.float32)).astype(jnp.bfloat16)
        total_grad = total_grad + jnp.dot(grad_rows.T, scaled, preferred_element_type=jnp.float32)
        row_norm_values.append(document_grad_norm)
    return (total_grad, jnp.stack(row_norm_values))
```

```python
import functools

import jax
import jax.numpy as jnp
from jax import lax
from jax.experimental import pallas as pl
from jax.experimental.pallas import tpu as pltpu
from jax.sharding import PartitionSpec as P

SPAN = 3


clip_norm = 128.0


def from_behind(block, axis, distance):
    devices = range(lax.axis_size(axis))
    route = [((i - distance) % len(devices), i) for i in devices]
    return lax.ppermute(block, axis, route)


def document_ids(lengths, offset, positions, all_tokens):
    doc_ends = jnp.cumsum(lengths)
    starts = doc_ends - lengths
    longest = jnp.argmax(lengths)
    labels = jnp.arange(lengths.shape[0], dtype=jnp.int32)
    doc_shift = jnp.sum(jnp.where(labels == longest, starts, 0)) + offset
    packed = (positions + doc_shift) % all_tokens
    return jnp.sum((doc_ends[None, :] <= packed[:, None]).astype(jnp.int32), axis=1)


def pair_terms(
    left_ids, left_inner, left_grad, right_ids, right_inner, right_grad, keep_rows, member
):
    inner_gram = jnp.einsum(
        "ir,jr->ij", left_inner, right_inner, preferred_element_type=jnp.float32
    )
    grad_gram = jnp.einsum("id,jd->ij", left_grad, right_grad, preferred_element_type=jnp.float32)
    same_doc = (left_ids[:, None] == right_ids[None, :]) & keep_rows[:, None]
    weight = jnp.sum(jnp.where(same_doc, inner_gram * grad_gram, 0.0), axis=1)
    return jnp.dot(weight, member, precision=lax.Precision.HIGHEST)


def boundary_crossing_plan(
    ids_of, local_document_index, adapter_inner, out_grad, member, my_block, block_rows, all_tokens
):
    first_doc = local_document_index[0]
    last_doc = local_document_index[block_rows - 1]
    before_id = ids_of(jnp.reshape((my_block * block_rows - 1) % all_tokens, (1,)))[0]
    after_id = ids_of(jnp.reshape((my_block + 1) * block_rows % all_tokens, (1,)))[0]
    starts_before = before_id == first_doc
    continues = after_id == last_doc
    crossing = starts_before & (local_document_index == first_doc) | continues & (
        local_document_index == last_doc
    )
    norm_terms = pair_terms(
        local_document_index,
        adapter_inner,
        out_grad,
        local_document_index,
        adapter_inner,
        out_grad,
        jnp.logical_not(crossing),
        member,
    )
    in_first = (local_document_index == first_doc).astype(jnp.bfloat16)
    in_last = (local_document_index == last_doc).astype(jnp.bfloat16)
    first_part = jnp.einsum(
        "tr,td->rd", adapter_inner * in_first[:, None], out_grad, preferred_element_type=jnp.float32
    )
    last_part = jnp.einsum(
        "tr,td->rd", adapter_inner * in_last[:, None], out_grad, preferred_element_type=jnp.float32
    )
    finish = (starts_before & jnp.logical_not((first_doc == last_doc) & continues)).astype(
        jnp.float32
    )
    return (first_doc, last_doc, starts_before, norm_terms, first_part, last_part, finish)


def chain_plan(out_grad, adapter_inner, doc_lengths, slab_offset, included):
    block_rows = out_grad.shape[0]
    ctx_size = lax.axis_size("ctx")
    my_block = lax.axis_index("ctx")
    all_tokens = ctx_size * block_rows
    lengths = doc_lengths[0]
    doc_count = lengths.shape[0]
    row_index = jnp.arange(block_rows, dtype=jnp.int32)
    labels = jnp.arange(doc_count, dtype=jnp.int32)

    def ids_of(positions):
        return document_ids(lengths, slab_offset[0], positions, all_tokens)

    local_document_index = ids_of(my_block * block_rows + row_index)
    member = (local_document_index[:, None] == labels[None, :]).astype(jnp.float32)
    first_doc, last_doc, starts_before, norm_terms, first_part, last_part, finish = (
        boundary_crossing_plan(
            ids_of,
            local_document_index,
            adapter_inner,
            out_grad,
            member,
            my_block,
            block_rows,
            all_tokens,
        )
    )
    chain_flag = (starts_before & (first_doc == last_doc)).astype(jnp.float32)
    running = last_part
    received = jnp.zeros_like(last_part)
    for distance in range(SPAN):
        received = from_behind(running, "ctx", 1)
        running = last_part + chain_flag * received
    complete_document = received + first_part
    end_term = finish * jnp.sum(complete_document * complete_document)
    norm_terms = norm_terms + end_term * (labels == first_doc).astype(jnp.float32)
    squares = lax.psum(norm_terms, "ctx")
    document_grad_norm = jnp.sqrt(squares)
    clip_factor = (
        included[0].astype(jnp.float32) * clip_norm / jnp.maximum(document_grad_norm, clip_norm)
    )
    token_factor = jnp.dot(member, clip_factor, precision=lax.Precision.HIGHEST)
    scaled = (token_factor[:, None] * adapter_inner.astype(jnp.float32)).astype(jnp.bfloat16)
    adapter_second_gradient = lax.psum_scatter(
        jnp.einsum("td,tr->dr", out_grad, scaled, preferred_element_type=jnp.float32),
        ("dp", "ctx"),
        scatter_dimension=0,
        tiled=True,
    )
    return (adapter_second_gradient, document_grad_norm[None, :])


def bits_of(n):
    return n.bit_length() - 1


def halving_orders(n_ctx):
    even = list(range(bits_of(n_ctx)))
    odd = list(even)
    if len(odd) >= 2:
        odd[0], odd[1] = odd[1], odd[0]
    return even, odd


def partials_kernel(
    n_dp, n_ctx, docs, len_ref, off_ref, inner_ref, grad_hbm, send_ref, keep_ref, grad_buf, spread, parts, sems
):
    rank, rows = inner_ref.shape
    span = grad_hbm.shape[1] // n_dp
    width = span // n_ctx
    copies = []
    for d in range(n_dp):
        copy = pltpu.make_async_copy(
            grad_hbm.at[:, pl.ds(d * span, span)], grad_buf.at[d], sems.at[d]
        )
        copy.start()
        copies.append(copy)
    me = lax.axis_index("ctx")
    odd = lax.rem(lax.axis_index("dp"), 2) == 1
    total = n_ctx * rows
    ends, starts = [], []
    running = jnp.int32(0)
    for k in range(docs):
        starts.append(running)
        running = running + len_ref[0, k]
        ends.append(running)
    longest, best = starts[0], len_ref[0, 0]
    for k in range(1, docs):
        better = len_ref[0, k] > best
        longest = jnp.where(better, starts[k], longest)
        best = jnp.where(better, len_ref[0, k], best)
    shift = longest + off_ref[0]
    packed = me * rows + shift + lax.broadcasted_iota(jnp.int32, (rank, rows), 1)
    packed = jnp.where(packed >= total, packed - total, packed)
    inner = inner_ref[...].astype(jnp.float32)
    for k in range(docs):
        inside = (packed >= starts[k]) & (packed < ends[k])
        spread[k * rank : (k + 1) * rank, :] = jnp.where(inside, inner, 0.0).astype(jnp.bfloat16)
    left = spread[...]
    even_order, odd_order = halving_orders(n_ctx)
    places = []
    for c in range(n_ctx):
        rel = me ^ c
        place_even = jnp.int32(0)
        place_odd = jnp.int32(0)
        for i in range(len(even_order)):
            weight = n_ctx >> (i + 1)
            place_even = place_even + ((rel >> even_order[i]) & 1) * weight
            place_odd = place_odd + ((rel >> odd_order[i]) & 1) * weight
        places.append(jnp.where(odd, place_odd, place_even))
    for d in range(n_dp):
        copies[d].wait()
        product = jnp.dot(left, grad_buf[d], preferred_element_type=jnp.float32)
        for c in range(n_ctx):
            parts[places[c], :, d * width : (d + 1) * width] = product[:, c * width : (c + 1) * width]
    half = n_ctx // 2
    keep_ref[...] = parts[0:half]
    send_ref[...] = parts[half:]


def norms_kernel(docs, rank, keep_ref, recv_ref, full_ref, square_ref):
    full = keep_ref[...] + recv_ref[...]
    full_ref[...] = full
    for k in range(docs):
        piece = full[k * rank : (k + 1) * rank]
        square_ref[k : k + 1, :] = jnp.broadcast_to(
            jnp.sum(piece * piece, keepdims=True), (1, square_ref.shape[1])
        )


def clip_kernel(n_dp, docs, rank, inc_ref, one_ref, two_ref, full_ref, send_ref, keep_ref, norm_ref):
    width = full_ref.shape[1] // n_dp
    lanes = lax.broadcasted_iota(jnp.int32, (1, one_ref.shape[1]), 1)
    norms = jnp.zeros((1, one_ref.shape[1]), jnp.float32)
    total = None
    for k in range(docs):
        norm = jnp.sqrt(one_ref[k : k + 1, :] + two_ref[k : k + 1, :])
        norms = jnp.where(lanes == k, norm, norms)
        factor = inc_ref[0, k].astype(jnp.float32) * clip_norm / jnp.maximum(norm, clip_norm)
        term = factor[:, 0:1] * full_ref[k * rank : (k + 1) * rank, :]
        total = term if total is None else total + term
    norm_ref[...] = norms[:, :docs]
    mine = lax.axis_index("dp")
    for d in range(n_dp):
        rel = mine ^ d
        piece = total[:, d * width : (d + 1) * width]

        @pl.when((rel & 1) == 1)
        def _():
            send_ref[rel >> 1] = piece

        @pl.when((rel & 1) == 0)
        def _():
            keep_ref[rel >> 1] = piece


def exchange(block, n_dp, n_ctx, even_bit, odd_bit):
    route = [
        (d * n_ctx + c, d * n_ctx + (c ^ (1 << (odd_bit if d % 2 else even_bit))))
        for d in range(n_dp)
        for c in range(n_ctx)
    ]
    return lax.ppermute(block, ("dp", "ctx"), route)


def swap_dp(block, n_dp, bit):
    return lax.ppermute(block, "dp", [(d, d ^ (1 << bit)) for d in range(n_dp)])


def dense_plan(out_grad, adapter_inner, doc_lengths, slab_offset, included):
    n_dp, n_ctx = lax.axis_size("dp"), lax.axis_size("ctx")
    rows, features = out_grad.shape
    rank = adapter_inner.shape[1]
    docs = doc_lengths.shape[1]
    high = docs * rank
    span = features // n_dp
    slab = features // n_ctx
    half = n_ctx // 2
    f32 = jnp.float32
    vmem = pl.BlockSpec(memory_space=pltpu.VMEM)
    smem = pl.BlockSpec(memory_space=pltpu.SMEM)
    send, keep = pl.pallas_call(
        functools.partial(partials_kernel, n_dp, n_ctx, docs),
        out_shape=[jax.ShapeDtypeStruct((half, high, slab), f32)] * 2,
        in_specs=[smem, smem, vmem, pl.BlockSpec(memory_space=pl.ANY)],
        out_specs=[vmem, vmem],
        scratch_shapes=[
            pltpu.VMEM((n_dp, rows, span), jnp.bfloat16),
            pltpu.VMEM((high, rows), jnp.bfloat16),
            pltpu.VMEM((n_ctx, high, slab), f32),
            pltpu.SemaphoreType.DMA((n_dp,)),
        ],
    )(doc_lengths, slab_offset, adapter_inner.T, out_grad)
    even, odd = halving_orders(n_ctx)
    rounds = list(zip(even, odd))
    for i, (e, o) in enumerate(rounds[:-1]):
        received = exchange(send, n_dp, n_ctx, e, o)
        half //= 2
        send = keep[half:] + received[half:]
        keep = keep[:half] + received[:half]
    received = exchange(send, n_dp, n_ctx, *rounds[-1])
    full, squares = pl.pallas_call(
        functools.partial(norms_kernel, docs, rank),
        out_shape=[
            jax.ShapeDtypeStruct((high, slab), f32),
            jax.ShapeDtypeStruct((docs, 128), f32),
        ],
        in_specs=[vmem, vmem],
        out_specs=[vmem, vmem],
    )(keep[0], received[0])
    for e, o in rounds[:-1]:
        squares = squares + exchange(squares, n_dp, n_ctx, e, o)
    other = exchange(squares, n_dp, n_ctx, *rounds[-1])
    width = slab // n_dp
    send, keep, norms = pl.pallas_call(
        functools.partial(clip_kernel, n_dp, docs, rank),
        out_shape=[
            jax.ShapeDtypeStruct((n_dp // 2, rank, width), f32),
            jax.ShapeDtypeStruct((n_dp // 2, rank, width), f32),
            jax.ShapeDtypeStruct((1, docs), f32),
        ],
        in_specs=[smem, vmem, vmem, vmem],
        out_specs=[vmem, vmem, vmem],
    )(included, squares, other, full)
    received = swap_dp(send, n_dp, 0)
    send = keep[1] + received[1]
    result = (keep[0] + received[0]) + swap_dp(send, n_dp, 1)
    return (result.T, norms)


def on_device(out_grad, adapter_inner, doc_lengths, slab_offset, included):
    n_dp, n_ctx = lax.axis_size("dp"), lax.axis_size("ctx")
    dense = (
        n_dp == 4
        and n_ctx >= 4
        and n_ctx & (n_ctx - 1) == 0
        and doc_lengths.shape[1] <= n_ctx
        and out_grad.shape[1] // n_dp % 128 == 0
    )
    plan = dense_plan if dense else chain_plan
    return plan(out_grad, adapter_inner, doc_lengths, slab_offset, included)


def solution(mesh):
    placed = (P(("dp", "ctx"), None), P(("dp", "ctx"), None), P("dp", None), P("dp"), P("dp", None))
    return jax.shard_map(
        on_device,
        mesh=mesh,
        in_specs=placed,
        out_specs=(P(("dp", "ctx"), None), P("dp", None)),
        check_vma=False,
    )
```

```python
import functools

import jax
import jax.numpy as jnp
from jax import lax
from jax.experimental import pallas as pl
from jax.experimental.pallas import tpu as pltpu
from jax.sharding import PartitionSpec as P

SPAN = 3


clip_norm = 128.0


def from_behind(block, axis, distance):
    devices = range(lax.axis_size(axis))
    route = [((i - distance) % len(devices), i) for i in devices]
    return lax.ppermute(block, axis, route)


def document_ids(lengths, offset, positions, all_tokens):
    doc_ends = jnp.cumsum(lengths)
    starts = doc_ends - lengths
    longest = jnp.argmax(lengths)
    labels = jnp.arange(lengths.shape[0], dtype=jnp.int32)
    doc_shift = jnp.sum(jnp.where(labels == longest, starts, 0)) + offset
    packed = (positions + doc_shift) % all_tokens
    return jnp.sum((doc_ends[None, :] <= packed[:, None]).astype(jnp.int32), axis=1)


def pair_terms(
    left_ids, left_inner, left_grad, right_ids, right_inner, right_grad, keep_rows, member
):
    inner_gram = jnp.einsum(
        "ir,jr->ij", left_inner, right_inner, preferred_element_type=jnp.float32
    )
    grad_gram = jnp.einsum("id,jd->ij", left_grad, right_grad, preferred_element_type=jnp.float32)
    same_doc = (left_ids[:, None] == right_ids[None, :]) & keep_rows[:, None]
    weight = jnp.sum(jnp.where(same_doc, inner_gram * grad_gram, 0.0), axis=1)
    return jnp.dot(weight, member, precision=lax.Precision.HIGHEST)


def boundary_crossing_plan(
    ids_of, local_document_index, adapter_inner, out_grad, member, my_block, block_rows, all_tokens
):
    first_doc = local_document_index[0]
    last_doc = local_document_index[block_rows - 1]
    before_id = ids_of(jnp.reshape((my_block * block_rows - 1) % all_tokens, (1,)))[0]
    after_id = ids_of(jnp.reshape((my_block + 1) * block_rows % all_tokens, (1,)))[0]
    starts_before = before_id == first_doc
    continues = after_id == last_doc
    crossing = starts_before & (local_document_index == first_doc) | continues & (
        local_document_index == last_doc
    )
    norm_terms = pair_terms(
        local_document_index,
        adapter_inner,
        out_grad,
        local_document_index,
        adapter_inner,
        out_grad,
        jnp.logical_not(crossing),
        member,
    )
    in_first = (local_document_index == first_doc).astype(jnp.bfloat16)
    in_last = (local_document_index == last_doc).astype(jnp.bfloat16)
    first_part = jnp.einsum(
        "tr,td->rd", adapter_inner * in_first[:, None], out_grad, preferred_element_type=jnp.float32
    )
    last_part = jnp.einsum(
        "tr,td->rd", adapter_inner * in_last[:, None], out_grad, preferred_element_type=jnp.float32
    )
    finish = (starts_before & jnp.logical_not((first_doc == last_doc) & continues)).astype(
        jnp.float32
    )
    return (first_doc, last_doc, starts_before, norm_terms, first_part, last_part, finish)


def chain_plan(out_grad, adapter_inner, doc_lengths, slab_offset, included):
    block_rows = out_grad.shape[0]
    ctx_size = lax.axis_size("ctx")
    my_block = lax.axis_index("ctx")
    all_tokens = ctx_size * block_rows
    lengths = doc_lengths[0]
    doc_count = lengths.shape[0]
    row_index = jnp.arange(block_rows, dtype=jnp.int32)
    labels = jnp.arange(doc_count, dtype=jnp.int32)

    def ids_of(positions):
        return document_ids(lengths, slab_offset[0], positions, all_tokens)

    local_document_index = ids_of(my_block * block_rows + row_index)
    member = (local_document_index[:, None] == labels[None, :]).astype(jnp.float32)
    first_doc, last_doc, starts_before, norm_terms, first_part, last_part, finish = (
        boundary_crossing_plan(
            ids_of,
            local_document_index,
            adapter_inner,
            out_grad,
            member,
            my_block,
            block_rows,
            all_tokens,
        )
    )
    chain_flag = (starts_before & (first_doc == last_doc)).astype(jnp.float32)
    running = last_part
    received = jnp.zeros_like(last_part)
    for distance in range(SPAN):
        received = from_behind(running, "ctx", 1)
        running = last_part + chain_flag * received
    complete_document = received + first_part
    end_term = finish * jnp.sum(complete_document * complete_document)
    norm_terms = norm_terms + end_term * (labels == first_doc).astype(jnp.float32)
    squares = lax.psum(norm_terms, "ctx")
    document_grad_norm = jnp.sqrt(squares)
    clip_factor = (
        included[0].astype(jnp.float32) * clip_norm / jnp.maximum(document_grad_norm, clip_norm)
    )
    token_factor = jnp.dot(member, clip_factor, precision=lax.Precision.HIGHEST)
    scaled = (token_factor[:, None] * adapter_inner.astype(jnp.float32)).astype(jnp.bfloat16)
    adapter_second_gradient = lax.psum_scatter(
        jnp.einsum("td,tr->dr", out_grad, scaled, preferred_element_type=jnp.float32),
        ("dp", "ctx"),
        scatter_dimension=0,
        tiled=True,
    )
    return (adapter_second_gradient, document_grad_norm[None, :])


def bits_of(n):
    return n.bit_length() - 1


def halving_orders(n_ctx):
    even = list(range(bits_of(n_ctx)))
    odd = list(even)
    odd[0], odd[1] = odd[1], odd[0]
    return even, odd


def my_bits(n_ctx):
    me = lax.axis_index("ctx")
    odd = lax.rem(lax.axis_index("dp"), 2) == 1
    even_order, odd_order = halving_orders(n_ctx)
    return [
        jnp.where(odd, (me >> o) & 1, (me >> e) & 1) for e, o in zip(even_order, odd_order)
    ]


def document_of(bits, flips):
    document = jnp.int32(0)
    for bit, flip in zip(bits, flips):
        document = document * 2 + (bit ^ flip)
    return document


def partials_kernel(
    flip, n_ctx, docs, chunks, len_ref, off_ref, inner_ref, grad_hbm, out_ref, grad_buf, spread, sems
):
    rank, rows = inner_ref.shape
    width = grad_hbm.shape[1] // chunks
    copies = []
    for j in range(chunks):
        copy = pltpu.make_async_copy(
            grad_hbm.at[:, pl.ds(j * width, width)], grad_buf.at[j], sems.at[j]
        )
        copy.start()
        copies.append(copy)
    total = n_ctx * rows
    running = jnp.int32(0)
    longest, best = jnp.int32(0), len_ref[0, 0]
    for k in range(1, docs):
        running = running + len_ref[0, k - 1]
        better = len_ref[0, k] > best
        longest = jnp.where(better, running, longest)
        best = jnp.where(better, len_ref[0, k], best)
    shift = longest + off_ref[0]
    packed = lax.axis_index("ctx") * rows + shift + lax.broadcasted_iota(jnp.int32, (rank, rows), 1)
    packed = jnp.where(packed >= total, packed - total, packed)
    inner = inner_ref[...].astype(jnp.float32)
    bits = my_bits(n_ctx)
    depth = bits_of(docs)
    places = docs // 2
    for place in range(places):
        flips = [flip] + [(place >> (depth - 2 - i)) & 1 for i in range(depth - 1)]
        document = document_of(bits[:depth], flips)
        start, length = jnp.int32(0), jnp.int32(0)
        for k in range(docs):
            start = start + jnp.where(k < document, len_ref[0, k], 0)
            length = length + jnp.where(k == document, len_ref[0, k], 0)
        inside = (packed >= start) & (packed < start + length)
        spread[place * rank : (place + 1) * rank, :] = jnp.where(inside, inner, 0.0).astype(
            jnp.bfloat16
        )
    left = spread[...]
    for j in range(chunks):
        copies[j].wait()
        product = jnp.dot(left, grad_buf[j], preferred_element_type=jnp.float32)
        for place in range(places):
            out_ref[place, :, j * width : (j + 1) * width] = product[
                place * rank : (place + 1) * rank
            ]


def clip_kernel(
    n_dp, n_ctx, docs, inc_ref, own_ref, mine_ref, other_ref, send_ref, keep_ref, norm_ref
):
    rank, features = own_ref.shape
    depth = bits_of(docs)
    span = features // n_dp
    slab = span // 2
    places = n_ctx // 2
    width = slab // places
    document = document_of(my_bits(n_ctx)[:depth], [0] * depth)
    flag = jnp.int32(0)
    for k in range(docs):
        flag = flag + jnp.where(k == document, inc_ref[0, k], 0)
    other = other_ref[...].astype(jnp.float32)
    whole = mine_ref[...].astype(jnp.float32) + other
    norm = jnp.sqrt(jnp.sum(whole * whole, keepdims=True))
    factor = flag.astype(jnp.float32) * clip_norm / jnp.maximum(norm, clip_norm)
    clipped = (own_ref[...] + other) * factor
    me = lax.axis_index("ctx")
    upper = me // places == 1
    low = lax.rem(me, places)
    dp = lax.axis_index("dp")
    core, chip = lax.rem(dp, 2), dp // 2
    halves = []
    for d in range(n_dp):
        base = d * span
        halves.append(
            jnp.where(
                upper, clipped[:, base + slab : base + span], clipped[:, base : base + slab]
            )
        )
    for target, ref in ((0, keep_ref), (1, send_ref)):
        for x in range(n_dp // 2):
            piece = jnp.where(core == target, halves[2 * x], halves[2 * x + 1])
            for q in range(places):
                ref[chip ^ x, low ^ q] = piece[:, q * width : (q + 1) * width]
    rows = lax.broadcasted_iota(jnp.int32, norm_ref.shape, 1)
    norm_ref[...] = jnp.where(rows == document, jnp.reshape(norm, (1, 1, 1)), 0.0)


def exchange(block, n_dp, n_ctx, even_bit, odd_bit):
    route = [
        (d * n_ctx + c, d * n_ctx + (c ^ (1 << (odd_bit if d % 2 else even_bit))))
        for d in range(n_dp)
        for c in range(n_ctx)
    ]
    return lax.ppermute(block, ("dp", "ctx"), route)


def swap_dp(block, n_dp, bit):
    return lax.ppermute(block, "dp", [(d, d ^ (1 << bit)) for d in range(n_dp)])


def halving_plan(out_grad, adapter_inner, doc_lengths, slab_offset, included):
    n_dp, n_ctx = lax.axis_size("dp"), lax.axis_size("ctx")
    rows, features = out_grad.shape
    rank = adapter_inner.shape[1]
    docs = doc_lengths.shape[1]
    f32 = jnp.float32
    vmem = pl.BlockSpec(memory_space=pltpu.VMEM)
    smem = pl.BlockSpec(memory_space=pltpu.SMEM)
    places = docs // 2
    chunks = max(1, features // 768)

    def partials(flip):
        return pl.pallas_call(
            functools.partial(partials_kernel, flip, n_ctx, docs, chunks),
            out_shape=jax.ShapeDtypeStruct((places, rank, features), f32),
            in_specs=[smem, smem, vmem, pl.BlockSpec(memory_space=pl.ANY)],
            out_specs=vmem,
            scratch_shapes=[
                pltpu.VMEM((chunks, rows, features // chunks), jnp.bfloat16),
                pltpu.VMEM((places * rank, rows), jnp.bfloat16),
                pltpu.SemaphoreType.DMA((chunks,)),
            ],
            cost_estimate=pl.CostEstimate(
                flops=2 * places * rank * rows * features,
                bytes_accessed=2 * rows * features,
                transcendentals=0,
            ),
        )(doc_lengths, slab_offset, adapter_inner.T, out_grad)

    even, odd = halving_orders(n_ctx)
    rounds = list(zip(even, odd))
    received = exchange(partials(1), n_dp, n_ctx, *rounds[0])
    keep = partials(0)
    for e, o in rounds[1:-1]:
        places //= 2
        send = keep[places:] + received[places:]
        keep = keep[:places] + received[:places]
        received = exchange(send, n_dp, n_ctx, e, o)
    own = keep[0] + received[0]
    mine = own.astype(jnp.bfloat16)
    other = exchange(mine, n_dp, n_ctx, *rounds[-1])
    places = n_ctx // 2
    width = features // (n_dp * n_ctx)
    pieces = jax.ShapeDtypeStruct((n_dp // 2, places, rank, width), f32)
    send, keep, norms = pl.pallas_call(
        functools.partial(clip_kernel, n_dp, n_ctx, docs),
        out_shape=[pieces, pieces, jax.ShapeDtypeStruct((1, rank, width), f32)],
        in_specs=[smem, vmem, vmem, vmem],
        out_specs=[vmem, vmem, vmem],
    )(included, own, mine, other)
    total = keep + swap_dp(send, n_dp, 0)
    total = total[0] + swap_dp(total[1], n_dp, 1)
    for bit in reversed(range(bits_of(places))):
        places //= 2
        received = exchange(jnp.concatenate([total[places:], norms]), n_dp, n_ctx, bit, bit)
        total = total[:places] + received[:places]
        norms = norms + received[places:]
    return (total[0].T, norms[:, :docs, 0])


def on_device(out_grad, adapter_inner, doc_lengths, slab_offset, included):
    n_dp, n_ctx = lax.axis_size("dp"), lax.axis_size("ctx")
    halving = (
        n_dp == 4
        and n_ctx >= 4
        and n_ctx & (n_ctx - 1) == 0
        and 2 * doc_lengths.shape[1] == n_ctx
        and doc_lengths.shape[1] <= adapter_inner.shape[1]
        and out_grad.shape[1] % 768 == 0
    )
    plan = halving_plan if halving else chain_plan
    return plan(out_grad, adapter_inner, doc_lengths, slab_offset, included)


def solution(mesh):
    placed = (P(("dp", "ctx"), None), P(("dp", "ctx"), None), P("dp", None), P("dp"), P("dp", None))
    return jax.shard_map(
        on_device,
        mesh=mesh,
        in_specs=placed,
        out_specs=(P(("dp", "ctx"), None), P("dp", None)),
        check_vma=False,
    )
```

```python
import functools

import jax
import jax.numpy as jnp
from jax import lax
from jax.experimental import pallas as pl
from jax.experimental.pallas import tpu as pltpu
from jax.sharding import PartitionSpec as P

SPAN = 3


clip_norm = 128.0


def from_behind(block, axis, distance):
    devices = range(lax.axis_size(axis))
    route = [((i - distance) % len(devices), i) for i in devices]
    return lax.ppermute(block, axis, route)


def document_ids(lengths, offset, positions, all_tokens):
    doc_ends = jnp.cumsum(lengths)
    starts = doc_ends - lengths
    longest = jnp.argmax(lengths)
    labels = jnp.arange(lengths.shape[0], dtype=jnp.int32)
    doc_shift = jnp.sum(jnp.where(labels == longest, starts, 0)) + offset
    packed = (positions + doc_shift) % all_tokens
    return jnp.sum((doc_ends[None, :] <= packed[:, None]).astype(jnp.int32), axis=1)


def pair_terms(
    left_ids, left_inner, left_grad, right_ids, right_inner, right_grad, keep_rows, member
):
    inner_gram = jnp.einsum(
        "ir,jr->ij", left_inner, right_inner, preferred_element_type=jnp.float32
    )
    grad_gram = jnp.einsum("id,jd->ij", left_grad, right_grad, preferred_element_type=jnp.float32)
    same_doc = (left_ids[:, None] == right_ids[None, :]) & keep_rows[:, None]
    weight = jnp.sum(jnp.where(same_doc, inner_gram * grad_gram, 0.0), axis=1)
    return jnp.dot(weight, member, precision=lax.Precision.HIGHEST)


def boundary_crossing_plan(
    ids_of, local_document_index, adapter_inner, out_grad, member, my_block, block_rows, all_tokens
):
    first_doc = local_document_index[0]
    last_doc = local_document_index[block_rows - 1]
    before_id = ids_of(jnp.reshape((my_block * block_rows - 1) % all_tokens, (1,)))[0]
    after_id = ids_of(jnp.reshape((my_block + 1) * block_rows % all_tokens, (1,)))[0]
    starts_before = before_id == first_doc
    continues = after_id == last_doc
    crossing = starts_before & (local_document_index == first_doc) | continues & (
        local_document_index == last_doc
    )
    norm_terms = pair_terms(
        local_document_index,
        adapter_inner,
        out_grad,
        local_document_index,
        adapter_inner,
        out_grad,
        jnp.logical_not(crossing),
        member,
    )
    in_first = (local_document_index == first_doc).astype(jnp.bfloat16)
    in_last = (local_document_index == last_doc).astype(jnp.bfloat16)
    first_part = jnp.einsum(
        "tr,td->rd", adapter_inner * in_first[:, None], out_grad, preferred_element_type=jnp.float32
    )
    last_part = jnp.einsum(
        "tr,td->rd", adapter_inner * in_last[:, None], out_grad, preferred_element_type=jnp.float32
    )
    finish = (starts_before & jnp.logical_not((first_doc == last_doc) & continues)).astype(
        jnp.float32
    )
    return (first_doc, last_doc, starts_before, norm_terms, first_part, last_part, finish)


def chain_plan(out_grad, adapter_inner, doc_lengths, slab_offset, included):
    block_rows = out_grad.shape[0]
    ctx_size = lax.axis_size("ctx")
    my_block = lax.axis_index("ctx")
    all_tokens = ctx_size * block_rows
    lengths = doc_lengths[0]
    doc_count = lengths.shape[0]
    row_index = jnp.arange(block_rows, dtype=jnp.int32)
    labels = jnp.arange(doc_count, dtype=jnp.int32)

    def ids_of(positions):
        return document_ids(lengths, slab_offset[0], positions, all_tokens)

    local_document_index = ids_of(my_block * block_rows + row_index)
    member = (local_document_index[:, None] == labels[None, :]).astype(jnp.float32)
    first_doc, last_doc, starts_before, norm_terms, first_part, last_part, finish = (
        boundary_crossing_plan(
            ids_of,
            local_document_index,
            adapter_inner,
            out_grad,
            member,
            my_block,
            block_rows,
            all_tokens,
        )
    )
    chain_flag = (starts_before & (first_doc == last_doc)).astype(jnp.float32)
    running = last_part
    received = jnp.zeros_like(last_part)
    for distance in range(SPAN):
        received = from_behind(running, "ctx", 1)
        running = last_part + chain_flag * received
    complete_document = received + first_part
    end_term = finish * jnp.sum(complete_document * complete_document)
    norm_terms = norm_terms + end_term * (labels == first_doc).astype(jnp.float32)
    squares = lax.psum(norm_terms, "ctx")
    document_grad_norm = jnp.sqrt(squares)
    clip_factor = (
        included[0].astype(jnp.float32) * clip_norm / jnp.maximum(document_grad_norm, clip_norm)
    )
    token_factor = jnp.dot(member, clip_factor, precision=lax.Precision.HIGHEST)
    scaled = (token_factor[:, None] * adapter_inner.astype(jnp.float32)).astype(jnp.bfloat16)
    adapter_second_gradient = lax.psum_scatter(
        jnp.einsum("td,tr->dr", out_grad, scaled, preferred_element_type=jnp.float32),
        ("dp", "ctx"),
        scatter_dimension=0,
        tiled=True,
    )
    return (adapter_second_gradient, document_grad_norm[None, :])


def bits_of(n):
    return n.bit_length() - 1


def halving_orders(n_ctx):
    even = list(range(bits_of(n_ctx)))
    odd = list(even)
    odd[0], odd[1] = odd[1], odd[0]
    return even, odd


def my_bits(n_ctx):
    me = lax.axis_index("ctx")
    odd = lax.rem(lax.axis_index("dp"), 2) == 1
    even_order, odd_order = halving_orders(n_ctx)
    return [
        jnp.where(odd, (me >> o) & 1, (me >> e) & 1) for e, o in zip(even_order, odd_order)
    ]


def document_of(bits, flips):
    document = jnp.int32(0)
    for bit, flip in zip(bits, flips):
        document = document * 2 + (bit ^ flip)
    return document


def partials_kernel(
    flip, n_ctx, docs, chunks, len_hbm, off_hbm, inner_hbm, grad_hbm, out_ref, grad_buf, inner_ref, spread, len_ref, off_ref, small_sems, sems
):
    rank, rows = inner_ref.shape
    width = grad_hbm.shape[1] // chunks
    small = [
        pltpu.make_async_copy(len_hbm, len_ref, small_sems.at[0]),
        pltpu.make_async_copy(off_hbm, off_ref, small_sems.at[1]),
        pltpu.make_async_copy(inner_hbm, inner_ref, small_sems.at[2]),
    ]
    copies = [
        pltpu.make_async_copy(
            grad_hbm.at[:, pl.ds(j * width, width)], grad_buf.at[j], sems.at[j]
        )
        for j in range(chunks)
    ]
    for copy in small + copies:
        copy.start()
    for copy in small:
        copy.wait()
    total = n_ctx * rows
    running = jnp.int32(0)
    longest, best = jnp.int32(0), len_ref[0, 0]
    for k in range(1, docs):
        running = running + len_ref[0, k - 1]
        better = len_ref[0, k] > best
        longest = jnp.where(better, running, longest)
        best = jnp.where(better, len_ref[0, k], best)
    shift = longest + off_ref[0]
    packed = lax.axis_index("ctx") * rows + shift + lax.broadcasted_iota(jnp.int32, (rank, rows), 1)
    packed = jnp.where(packed >= total, packed - total, packed)
    inner = inner_ref[...].astype(jnp.float32)
    bits = my_bits(n_ctx)
    depth = bits_of(docs)
    places = docs // 2
    for place in range(places):
        flips = [flip] + [(place >> (depth - 2 - i)) & 1 for i in range(depth - 1)]
        document = document_of(bits[:depth], flips)
        start, length = jnp.int32(0), jnp.int32(0)
        for k in range(docs):
            start = start + jnp.where(k < document, len_ref[0, k], 0)
            length = length + jnp.where(k == document, len_ref[0, k], 0)
        inside = (packed >= start) & (packed < start + length)
        spread[place * rank : (place + 1) * rank, :] = jnp.where(inside, inner, 0.0).astype(
            jnp.bfloat16
        )
    left = spread[...]
    for j in range(chunks):
        copies[j].wait()
        product = jnp.dot(left, grad_buf[j], preferred_element_type=jnp.float32)
        for place in range(places):
            out_ref[place, :, j * width : (j + 1) * width] = product[
                place * rank : (place + 1) * rank
            ]


def fold_kernel(keep_ref, recv_ref, send_ref, left_ref):
    half = keep_ref.shape[0] // 2
    send_ref[...] = keep_ref[half:] + recv_ref[half:]
    left_ref[...] = keep_ref[:half] + recv_ref[:half]


def round_kernel(keep_ref, recv_ref, own_ref, mine_ref):
    own = keep_ref[0] + recv_ref[0]
    own_ref[...] = own
    mine_ref[...] = own.astype(jnp.bfloat16)


def swapped(pieces, bit):
    half = len(pieces) // 2
    low, high = pieces[:half], pieces[half:]
    first = [jnp.where(bit == 1, b, a) for a, b in zip(low, high)]
    second = [jnp.where(bit == 1, a, b) for a, b in zip(low, high)]
    return first, second


def relative(pieces, low):
    if len(pieces) == 1:
        return pieces
    first, second = swapped(pieces, (low >> (bits_of(len(pieces)) - 1)) & 1)
    return relative(first, low) + relative(second, low)


def clip_kernel(
    n_dp, n_ctx, docs, inc_ref, own_ref, mine_ref, other_ref, send_ref, keep_ref, norm_ref
):
    rank, features = own_ref.shape
    depth = bits_of(docs)
    span = features // n_dp
    slab = span // 2
    places = n_ctx // 2
    width = slab // places
    document = document_of(my_bits(n_ctx)[:depth], [0] * depth)
    flag = jnp.int32(0)
    for k in range(docs):
        flag = flag + jnp.where(k == document, inc_ref[0, k], 0)
    other = other_ref[...].astype(jnp.float32)
    whole = mine_ref[...].astype(jnp.float32) + other
    norm = jnp.sqrt(jnp.sum(whole * whole, keepdims=True))
    factor = flag.astype(jnp.float32) * clip_norm / jnp.maximum(norm, clip_norm)
    clipped = (own_ref[...] + other) * factor
    me = lax.axis_index("ctx")
    upper = me // places == 1
    low = lax.rem(me, places)
    dp = lax.axis_index("dp")
    core, chip = lax.rem(dp, 2), dp // 2
    halves = []
    for d in range(n_dp):
        base = d * span
        halves.append(
            jnp.where(
                upper, clipped[:, base + slab : base + span], clipped[:, base : base + slab]
            )
        )
    for target, ref in ((0, keep_ref), (1, send_ref)):
        for x in range(n_dp // 2):
            piece = jnp.where(core == target, halves[2 * x], halves[2 * x + 1])
            pieces = relative([piece[:, q * width : (q + 1) * width] for q in range(places)], low)
            ref[chip ^ x] = jnp.concatenate(pieces, axis=1)
    rows = lax.broadcasted_iota(jnp.int32, norm_ref.shape, 0)
    norm_ref[...] = jnp.where(rows == document, norm, 0.0)


def core_kernel(keep_ref, recv_ref, send_ref):
    send_ref[...] = keep_ref[1] + recv_ref[1]


def with_norms(block, norms, send_ref):
    width = block.shape[1]
    spare = send_ref.shape[1] - width
    send_ref[...] = jnp.concatenate([block, norms[:, :spare]], axis=1)


def chip_kernel(keep_ref, core_ref, recv_ref, norm_ref, send_ref, left_ref):
    total = keep_ref[0] + core_ref[0] + recv_ref[...]
    half = total.shape[1] // 2
    left_ref[...] = total[:, :half]
    with_norms(total[:, half:], norm_ref[...], send_ref)


def step_kernel(keep_ref, recv_ref, norm_ref, send_ref, left_ref, norms_ref):
    width = keep_ref.shape[1]
    half = width // 2
    received = recv_ref[...]
    total = keep_ref[...] + received[:, :width]
    norms = norm_ref[...] + received[:, width : width + 1]
    left_ref[...] = total[:, :half]
    norms_ref[...] = norms
    with_norms(total[:, half:], norms, send_ref)


def last_kernel(docs, keep_ref, recv_ref, norm_ref, out_ref, norms_ref):
    width = keep_ref.shape[1]
    received = recv_ref[...]
    out_ref[...] = keep_ref[...] + received[:, :width]
    norms = norm_ref[...] + received[:, width : width + 1]
    rows = lax.broadcasted_iota(jnp.int32, norms.shape, 0)
    lanes = lax.broadcasted_iota(jnp.int32, norms.shape, 1)
    norms_ref[...] = jnp.sum(jnp.where(rows == lanes, norms, 0.0), axis=0, keepdims=True)[:, :docs]


def exchange(block, n_dp, n_ctx, even_bit, odd_bit):
    route = [
        (d * n_ctx + c, d * n_ctx + (c ^ (1 << (odd_bit if d % 2 else even_bit))))
        for d in range(n_dp)
        for c in range(n_ctx)
    ]
    return lax.ppermute(block, ("dp", "ctx"), route)


def swap_dp(block, n_dp, bit):
    return lax.ppermute(block, "dp", [(d, d ^ (1 << bit)) for d in range(n_dp)])


def in_vmem(kernel, shapes, *operands, scalars=()):
    vmem = pl.BlockSpec(memory_space=pltpu.VMEM)
    smem = pl.BlockSpec(memory_space=pltpu.SMEM)
    return pl.pallas_call(
        kernel,
        out_shape=[pltpu.VMEM(shape, dtype) for shape, dtype in shapes],
        in_specs=[smem] * len(scalars) + [vmem] * len(operands),
        out_specs=[vmem] * len(shapes),
    )(*scalars, *[pltpu.with_memory_space_constraint(x, pltpu.VMEM) for x in operands])


def halving_plan(out_grad, adapter_inner, doc_lengths, slab_offset, included):
    n_dp, n_ctx = lax.axis_size("dp"), lax.axis_size("ctx")
    rows, features = out_grad.shape
    rank = adapter_inner.shape[1]
    docs = doc_lengths.shape[1]
    f32 = jnp.float32
    vmem = pl.BlockSpec(memory_space=pltpu.VMEM)
    hbm = pl.BlockSpec(memory_space=pl.ANY)
    places = docs // 2
    chunks = max(1, features // 768)

    def partials(flip):
        return pl.pallas_call(
            functools.partial(partials_kernel, flip, n_ctx, docs, chunks),
            out_shape=pltpu.VMEM((places, rank, features), f32),
            in_specs=[hbm, hbm, hbm, hbm],
            out_specs=vmem,
            scratch_shapes=[
                pltpu.VMEM((chunks, rows, features // chunks), jnp.bfloat16),
                pltpu.VMEM((rank, rows), jnp.bfloat16),
                pltpu.VMEM((places * rank, rows), jnp.bfloat16),
                pltpu.SMEM(doc_lengths.shape, jnp.int32),
                pltpu.SMEM(slab_offset.shape, jnp.int32),
                pltpu.SemaphoreType.DMA((3,)),
                pltpu.SemaphoreType.DMA((chunks,)),
            ],
            cost_estimate=pl.CostEstimate(
                flops=2 * places * rank * rows * features,
                bytes_accessed=2 * rows * features,
                transcendentals=0,
            ),
        )(doc_lengths, slab_offset, adapter_inner.T, out_grad)

    even, odd = halving_orders(n_ctx)
    rounds = list(zip(even, odd))
    received = exchange(partials(1), n_dp, n_ctx, *rounds[0])
    keep = partials(0)
    for e, o in rounds[1:-1]:
        places //= 2
        shape = ((places, rank, features), f32)
        send, keep = in_vmem(fold_kernel, [shape, shape], keep, received)
        received = exchange(send, n_dp, n_ctx, e, o)
    own, mine = in_vmem(
        round_kernel,
        [((rank, features), f32), ((rank, features), jnp.bfloat16)],
        keep,
        received,
    )
    other = exchange(mine, n_dp, n_ctx, *rounds[-1])
    slab = features // (2 * n_dp)
    pieces = ((n_dp // 2, rank, slab), f32)
    column = ((rank, 128), f32)
    send, keep, norms = in_vmem(
        functools.partial(clip_kernel, n_dp, n_ctx, docs),
        [pieces, pieces, column],
        own,
        mine,
        other,
        scalars=(included,),
    )
    core = swap_dp(send, n_dp, 0)
    (send,) = in_vmem(core_kernel, [((rank, slab), f32)], keep, core)
    received = swap_dp(send, n_dp, 1)

    def shapes(width):
        return [((rank, width // 128 * 128 + 128), f32), ((rank, width), f32)]

    width = slab // 2
    steps = list(reversed(range(bits_of(n_ctx // 2))))
    send, keep = in_vmem(chip_kernel, shapes(width), keep, core, received, norms)
    for bit in steps[:-1]:
        width //= 2
        received = exchange(send, n_dp, n_ctx, bit, bit)
        send, keep, norms = in_vmem(step_kernel, shapes(width) + [column], keep, received, norms)
    received = exchange(send, n_dp, n_ctx, steps[-1], steps[-1])
    result, norms = pl.pallas_call(
        functools.partial(last_kernel, docs),
        out_shape=[
            jax.ShapeDtypeStruct((rank, width), f32),
            jax.ShapeDtypeStruct((1, docs), f32),
        ],
        in_specs=[vmem] * 3,
        out_specs=[vmem, vmem],
    )(*[pltpu.with_memory_space_constraint(x, pltpu.VMEM) for x in (keep, received, norms)])
    return (result.T, norms)


def on_device(out_grad, adapter_inner, doc_lengths, slab_offset, included):
    n_dp, n_ctx = lax.axis_size("dp"), lax.axis_size("ctx")
    halving = (
        n_dp == 4
        and n_ctx >= 4
        and n_ctx & (n_ctx - 1) == 0
        and 2 * doc_lengths.shape[1] == n_ctx
        and doc_lengths.shape[1] <= adapter_inner.shape[1]
        and out_grad.shape[1] % 768 == 0
    )
    plan = halving_plan if halving else chain_plan
    return plan(out_grad, adapter_inner, doc_lengths, slab_offset, included)


def solution(mesh):
    placed = (P(("dp", "ctx"), None), P(("dp", "ctx"), None), P("dp", None), P("dp"), P("dp", None))
    return jax.shard_map(
        on_device,
        mesh=mesh,
        in_specs=placed,
        out_specs=(P(("dp", "ctx"), None), P("dp", None)),
        check_vma=False,
    )
```

```python
import functools

import jax
import jax.numpy as jnp
from jax import lax
from jax.experimental import pallas as pl
from jax.experimental.pallas import tpu as pltpu
from jax.sharding import PartitionSpec as P

SPAN = 3
PARTS = 2


clip_norm = 128.0


def from_behind(block, axis, distance):
    devices = range(lax.axis_size(axis))
    route = [((i - distance) % len(devices), i) for i in devices]
    return lax.ppermute(block, axis, route)


def document_ids(lengths, offset, positions, all_tokens):
    doc_ends = jnp.cumsum(lengths)
    starts = doc_ends - lengths
    longest = jnp.argmax(lengths)
    labels = jnp.arange(lengths.shape[0], dtype=jnp.int32)
    doc_shift = jnp.sum(jnp.where(labels == longest, starts, 0)) + offset
    packed = (positions + doc_shift) % all_tokens
    return jnp.sum((doc_ends[None, :] <= packed[:, None]).astype(jnp.int32), axis=1)


def pair_terms(
    left_ids, left_inner, left_grad, right_ids, right_inner, right_grad, keep_rows, member
):
    inner_gram = jnp.einsum(
        "ir,jr->ij", left_inner, right_inner, preferred_element_type=jnp.float32
    )
    grad_gram = jnp.einsum("id,jd->ij", left_grad, right_grad, preferred_element_type=jnp.float32)
    same_doc = (left_ids[:, None] == right_ids[None, :]) & keep_rows[:, None]
    weight = jnp.sum(jnp.where(same_doc, inner_gram * grad_gram, 0.0), axis=1)
    return jnp.dot(weight, member, precision=lax.Precision.HIGHEST)


def boundary_crossing_plan(
    ids_of, local_document_index, adapter_inner, out_grad, member, my_block, block_rows, all_tokens
):
    first_doc = local_document_index[0]
    last_doc = local_document_index[block_rows - 1]
    before_id = ids_of(jnp.reshape((my_block * block_rows - 1) % all_tokens, (1,)))[0]
    after_id = ids_of(jnp.reshape((my_block + 1) * block_rows % all_tokens, (1,)))[0]
    starts_before = before_id == first_doc
    continues = after_id == last_doc
    crossing = starts_before & (local_document_index == first_doc) | continues & (
        local_document_index == last_doc
    )
    norm_terms = pair_terms(
        local_document_index,
        adapter_inner,
        out_grad,
        local_document_index,
        adapter_inner,
        out_grad,
        jnp.logical_not(crossing),
        member,
    )
    in_first = (local_document_index == first_doc).astype(jnp.bfloat16)
    in_last = (local_document_index == last_doc).astype(jnp.bfloat16)
    first_part = jnp.einsum(
        "tr,td->rd", adapter_inner * in_first[:, None], out_grad, preferred_element_type=jnp.float32
    )
    last_part = jnp.einsum(
        "tr,td->rd", adapter_inner * in_last[:, None], out_grad, preferred_element_type=jnp.float32
    )
    finish = (starts_before & jnp.logical_not((first_doc == last_doc) & continues)).astype(
        jnp.float32
    )
    return (first_doc, last_doc, starts_before, norm_terms, first_part, last_part, finish)


def chain_plan(out_grad, adapter_inner, doc_lengths, slab_offset, included):
    block_rows = out_grad.shape[0]
    ctx_size = lax.axis_size("ctx")
    my_block = lax.axis_index("ctx")
    all_tokens = ctx_size * block_rows
    lengths = doc_lengths[0]
    doc_count = lengths.shape[0]
    row_index = jnp.arange(block_rows, dtype=jnp.int32)
    labels = jnp.arange(doc_count, dtype=jnp.int32)

    def ids_of(positions):
        return document_ids(lengths, slab_offset[0], positions, all_tokens)

    local_document_index = ids_of(my_block * block_rows + row_index)
    member = (local_document_index[:, None] == labels[None, :]).astype(jnp.float32)
    first_doc, last_doc, starts_before, norm_terms, first_part, last_part, finish = (
        boundary_crossing_plan(
            ids_of,
            local_document_index,
            adapter_inner,
            out_grad,
            member,
            my_block,
            block_rows,
            all_tokens,
        )
    )
    chain_flag = (starts_before & (first_doc == last_doc)).astype(jnp.float32)
    running = last_part
    received = jnp.zeros_like(last_part)
    for distance in range(SPAN):
        received = from_behind(running, "ctx", 1)
        running = last_part + chain_flag * received
    complete_document = received + first_part
    end_term = finish * jnp.sum(complete_document * complete_document)
    norm_terms = norm_terms + end_term * (labels == first_doc).astype(jnp.float32)
    squares = lax.psum(norm_terms, "ctx")
    document_grad_norm = jnp.sqrt(squares)
    clip_factor = (
        included[0].astype(jnp.float32) * clip_norm / jnp.maximum(document_grad_norm, clip_norm)
    )
    token_factor = jnp.dot(member, clip_factor, precision=lax.Precision.HIGHEST)
    scaled = (token_factor[:, None] * adapter_inner.astype(jnp.float32)).astype(jnp.bfloat16)
    adapter_second_gradient = lax.psum_scatter(
        jnp.einsum("td,tr->dr", out_grad, scaled, preferred_element_type=jnp.float32),
        ("dp", "ctx"),
        scatter_dimension=0,
        tiled=True,
    )
    return (adapter_second_gradient, document_grad_norm[None, :])


def bits_of(n):
    return n.bit_length() - 1


def halving_orders(n_ctx):
    even = list(range(bits_of(n_ctx)))
    odd = list(even)
    odd[0], odd[1] = odd[1], odd[0]
    return even, odd


def my_bits(n_ctx):
    me = lax.axis_index("ctx")
    odd = lax.rem(lax.axis_index("dp"), 2) == 1
    even_order, odd_order = halving_orders(n_ctx)
    return [
        jnp.where(odd, (me >> o) & 1, (me >> e) & 1) for e, o in zip(even_order, odd_order)
    ]


def document_of(bits, flips):
    document = jnp.int32(0)
    for bit, flip in zip(bits, flips):
        document = document * 2 + (bit ^ flip)
    return document


def partials_kernel(
    half, n_ctx, docs, chunks, len_hbm, off_hbm, inc_hbm, inner_hbm, grad_hbm, *refs
):
    send_ref, keep_ref, flag_ref, grad_buf, inner_ref, spread = refs[:6]
    len_ref, off_ref, inc_ref, small_sems, sems = refs[6:]
    rank, rows = inner_ref.shape
    features = send_ref.shape[2]
    width = features // chunks
    small = [
        pltpu.make_async_copy(len_hbm, len_ref, small_sems.at[0]),
        pltpu.make_async_copy(off_hbm, off_ref, small_sems.at[1]),
        pltpu.make_async_copy(inner_hbm, inner_ref, small_sems.at[2]),
        pltpu.make_async_copy(inc_hbm, inc_ref, small_sems.at[3]),
    ]
    copies = [
        pltpu.make_async_copy(
            grad_hbm.at[:, pl.ds(half * features + j * width, width)], grad_buf.at[j], sems.at[j]
        )
        for j in range(chunks)
    ]
    for copy in small + copies:
        copy.start()
    for copy in small:
        copy.wait()
    total = n_ctx * rows
    running = jnp.int32(0)
    longest, best = jnp.int32(0), len_ref[0, 0]
    for k in range(1, docs):
        running = running + len_ref[0, k - 1]
        better = len_ref[0, k] > best
        longest = jnp.where(better, running, longest)
        best = jnp.where(better, len_ref[0, k], best)
    shift = longest + off_ref[0, 0]
    packed = lax.axis_index("ctx") * rows + shift + lax.broadcasted_iota(jnp.int32, (rank, rows), 1)
    packed = jnp.where(packed >= total, packed - total, packed)
    inner = inner_ref[...].astype(jnp.float32)
    depth = bits_of(docs)
    bits = my_bits(n_ctx)[:depth]
    for place in range(docs):
        document = document_of(bits, [(place >> (depth - 1 - i)) & 1 for i in range(depth)])
        start, length, flag = jnp.int32(0), jnp.int32(0), jnp.int32(0)
        for k in range(docs):
            start = start + jnp.where(k < document, len_ref[0, k], 0)
            length = length + jnp.where(k == document, len_ref[0, k], 0)
            flag = flag + jnp.where(k == document, inc_ref[0, k], 0)
        inside = (packed >= start) & (packed < start + length)
        spread[place * rank : (place + 1) * rank, :] = jnp.where(inside, inner, 0.0).astype(
            jnp.bfloat16
        )
        if place == 0:
            flag_ref[...] = jnp.full(flag_ref.shape, flag.astype(jnp.float32))
    left = spread[...]
    for j in range(chunks):
        copies[j].wait()
        product = jnp.dot(left, grad_buf[j], preferred_element_type=jnp.float32)
        for place in range(docs):
            ref = keep_ref if place < docs // 2 else send_ref
            ref[place % (docs // 2), :, j * width : (j + 1) * width] = product[
                place * rank : (place + 1) * rank
            ]


def fold_kernel(keep_ref, recv_ref, send_ref, left_ref):
    half = keep_ref.shape[0] // 2
    send_ref[...] = keep_ref[half:] + recv_ref[half:]
    left_ref[...] = keep_ref[:half] + recv_ref[:half]


def round_kernel(keep_ref, recv_ref, own_ref, mine_ref):
    own = keep_ref[0] + recv_ref[0]
    own_ref[...] = own
    mine_ref[...] = own.astype(jnp.bfloat16)


def swapped(pieces, bit):
    half = len(pieces) // 2
    low, high = pieces[:half], pieces[half:]
    first = [jnp.where(bit == 1, b, a) for a, b in zip(low, high)]
    second = [jnp.where(bit == 1, a, b) for a, b in zip(low, high)]
    return first, second


def relative(pieces, low):
    if len(pieces) == 1:
        return pieces
    first, second = swapped(pieces, (low >> (bits_of(len(pieces)) - 1)) & 1)
    return relative(first, low) + relative(second, low)


def clip_kernel(n_dp, n_ctx, docs, parts, *refs):
    own_refs, mine_refs, other_refs = refs[:parts], refs[parts : 2 * parts], refs[2 * parts : 3 * parts]
    flag_ref, send_ref, keep_ref, norm_ref = refs[3 * parts :]
    depth = bits_of(docs)
    slab = send_ref.shape[2]
    span = 2 * slab
    places = n_ctx // 2
    width = slab // places
    square = None
    wholes = []
    for own_ref, mine_ref, other_ref in zip(own_refs, mine_refs, other_refs):
        other = other_ref[...].astype(jnp.float32)
        whole = mine_ref[...].astype(jnp.float32) + other
        wholes.append(own_ref[...] + other)
        term = jnp.sum(whole * whole, keepdims=True)
        square = term if square is None else square + term
    norm = jnp.sqrt(square)
    factor = flag_ref[0:1, 0:1] * clip_norm / jnp.maximum(norm, clip_norm)
    me = lax.axis_index("ctx")
    upper = me // places == 1
    low = lax.rem(me, places)
    dp = lax.axis_index("dp")
    core, chip = lax.rem(dp, 2), dp // 2
    halves = []
    for d in range(n_dp):
        whole = wholes[d * parts // n_dp]
        base = d % (n_dp // parts) * span
        halves.append(
            jnp.where(upper, whole[:, base + slab : base + span], whole[:, base : base + slab])
            * factor
        )
    for target, ref in ((0, keep_ref), (1, send_ref)):
        for x in range(n_dp // 2):
            piece = jnp.where(core == target, halves[2 * x], halves[2 * x + 1])
            pieces = relative([piece[:, q * width : (q + 1) * width] for q in range(places)], low)
            ref[chip ^ x] = jnp.concatenate(pieces, axis=1)
    document = document_of(my_bits(n_ctx)[:depth], [0] * depth)
    rows = lax.broadcasted_iota(jnp.int32, norm_ref.shape, 0)
    norm_ref[...] = jnp.where(rows == document, norm, 0.0)


def core_kernel(keep_ref, recv_ref, send_ref):
    send_ref[...] = keep_ref[1] + recv_ref[1]


def with_norms(block, norms, send_ref):
    width = block.shape[1]
    spare = send_ref.shape[1] - width
    send_ref[...] = jnp.concatenate([block, norms[:, :spare]], axis=1)


def chip_kernel(keep_ref, core_ref, recv_ref, norm_ref, send_ref, left_ref):
    total = keep_ref[0] + core_ref[0] + recv_ref[...]
    half = total.shape[1] // 2
    left_ref[...] = total[:, :half]
    with_norms(total[:, half:], norm_ref[...], send_ref)


def step_kernel(keep_ref, recv_ref, norm_ref, send_ref, left_ref, norms_ref):
    width = keep_ref.shape[1]
    half = width // 2
    received = recv_ref[...]
    total = keep_ref[...] + received[:, :width]
    norms = norm_ref[...] + received[:, width : width + 1]
    left_ref[...] = total[:, :half]
    norms_ref[...] = norms
    with_norms(total[:, half:], norms, send_ref)


def last_kernel(docs, keep_ref, recv_ref, norm_ref, out_ref, norms_ref):
    width = keep_ref.shape[1]
    received = recv_ref[...]
    out_ref[...] = keep_ref[...] + received[:, :width]
    norms = norm_ref[...] + received[:, width : width + 1]
    rows = lax.broadcasted_iota(jnp.int32, norms.shape, 0)
    lanes = lax.broadcasted_iota(jnp.int32, norms.shape, 1)
    norms_ref[...] = jnp.sum(jnp.where(rows == lanes, norms, 0.0), axis=0, keepdims=True)[:, :docs]


def exchange(block, n_dp, n_ctx, even_bit, odd_bit):
    route = [
        (d * n_ctx + c, d * n_ctx + (c ^ (1 << (odd_bit if d % 2 else even_bit))))
        for d in range(n_dp)
        for c in range(n_ctx)
    ]
    return lax.ppermute(block, ("dp", "ctx"), route)


def swap_dp(block, n_dp, bit):
    return lax.ppermute(block, "dp", [(d, d ^ (1 << bit)) for d in range(n_dp)])


def in_vmem(kernel, shapes, *operands, scalars=()):
    vmem = pl.BlockSpec(memory_space=pltpu.VMEM)
    smem = pl.BlockSpec(memory_space=pltpu.SMEM)
    return pl.pallas_call(
        kernel,
        out_shape=[pltpu.VMEM(shape, dtype) for shape, dtype in shapes],
        in_specs=[smem] * len(scalars) + [vmem] * len(operands),
        out_specs=[vmem] * len(shapes),
    )(*scalars, *[pltpu.with_memory_space_constraint(x, pltpu.VMEM) for x in operands])


def halving_plan(out_grad, adapter_inner, doc_lengths, slab_offset, included):
    n_dp, n_ctx = lax.axis_size("dp"), lax.axis_size("ctx")
    rows, features = out_grad.shape
    rank = adapter_inner.shape[1]
    docs = doc_lengths.shape[1]
    f32 = jnp.float32
    vmem = pl.BlockSpec(memory_space=pltpu.VMEM)
    hbm = pl.BlockSpec(memory_space=pl.ANY)
    parts = PARTS
    part = features // parts
    chunks = max(1, part // 768)
    block = pltpu.VMEM((docs // 2, rank, part), f32)
    column = ((rank, 128), f32)

    def partials(half):
        return pl.pallas_call(
            functools.partial(partials_kernel, half, n_ctx, docs, chunks),
            out_shape=[block, block, pltpu.VMEM(*column)],
            in_specs=[hbm] * 5,
            out_specs=[vmem] * 3,
            scratch_shapes=[
                pltpu.VMEM((chunks, rows, part // chunks), jnp.bfloat16),
                pltpu.VMEM((rank, rows), jnp.bfloat16),
                pltpu.VMEM((docs * rank, rows), jnp.bfloat16),
                pltpu.SMEM(doc_lengths.shape, jnp.int32),
                pltpu.SMEM((1, 1), jnp.int32),
                pltpu.SMEM(included.shape, jnp.int32),
                pltpu.SemaphoreType.DMA((4,)),
                pltpu.SemaphoreType.DMA((chunks,)),
            ],
            cost_estimate=pl.CostEstimate(
                flops=2 * docs * rank * rows * part,
                bytes_accessed=2 * rows * part,
                transcendentals=0,
            ),
        )(doc_lengths, slab_offset[:, None], included, adapter_inner.T, out_grad)

    even, odd = halving_orders(n_ctx)
    rounds = list(zip(even, odd))
    owns, mines, others = [], [], []
    for half in range(parts):
        send, keep, flag = partials(half)
        received = exchange(send, n_dp, n_ctx, *rounds[0])
        places = docs // 2
        for e, o in rounds[1:-1]:
            places //= 2
            shape = ((places, rank, part), f32)
            send, keep = in_vmem(fold_kernel, [shape, shape], keep, received)
            received = exchange(send, n_dp, n_ctx, e, o)
        own, mine = in_vmem(
            round_kernel, [((rank, part), f32), ((rank, part), jnp.bfloat16)], keep, received
        )
        owns.append(own)
        mines.append(mine)
        others.append(exchange(mine, n_dp, n_ctx, *rounds[-1]))
    slab = features // (2 * n_dp)
    pieces = ((n_dp // 2, rank, slab), f32)
    send, keep, norms = in_vmem(
        functools.partial(clip_kernel, n_dp, n_ctx, docs, parts),
        [pieces, pieces, column],
        *owns,
        *mines,
        *others,
        flag,
    )
    core = swap_dp(send, n_dp, 0)
    (send,) = in_vmem(core_kernel, [((rank, slab), f32)], keep, core)
    received = swap_dp(send, n_dp, 1)

    def shapes(width):
        return [((rank, width // 128 * 128 + 128), f32), ((rank, width), f32)]

    width = slab // 2
    steps = list(reversed(range(bits_of(n_ctx // 2))))
    send, keep = in_vmem(chip_kernel, shapes(width), keep, core, received, norms)
    for bit in steps[:-1]:
        width //= 2
        received = exchange(send, n_dp, n_ctx, bit, bit)
        send, keep, norms = in_vmem(step_kernel, shapes(width) + [column], keep, received, norms)
    received = exchange(send, n_dp, n_ctx, steps[-1], steps[-1])
    result, norms = pl.pallas_call(
        functools.partial(last_kernel, docs),
        out_shape=[
            jax.ShapeDtypeStruct((rank, width), f32),
            jax.ShapeDtypeStruct((1, docs), f32),
        ],
        in_specs=[vmem] * 3,
        out_specs=[vmem, vmem],
    )(*[pltpu.with_memory_space_constraint(x, pltpu.VMEM) for x in (keep, received, norms)])
    return (result.T, norms)


def on_device(out_grad, adapter_inner, doc_lengths, slab_offset, included):
    n_dp, n_ctx = lax.axis_size("dp"), lax.axis_size("ctx")
    halving = (
        n_dp == 4
        and n_ctx >= 4
        and n_ctx & (n_ctx - 1) == 0
        and 2 * doc_lengths.shape[1] == n_ctx
        and doc_lengths.shape[1] <= adapter_inner.shape[1]
        and out_grad.shape[1] % (768 * PARTS) == 0
    )
    plan = halving_plan if halving else chain_plan
    return plan(out_grad, adapter_inner, doc_lengths, slab_offset, included)


def solution(mesh):
    placed = (P(("dp", "ctx"), None), P(("dp", "ctx"), None), P("dp", None), P("dp"), P("dp", None))
    return jax.shard_map(
        on_device,
        mesh=mesh,
        in_specs=placed,
        out_specs=(P(("dp", "ctx"), None), P("dp", None)),
        check_vma=False,
    )
```

```python
import functools

import jax
import jax.numpy as jnp
from jax import lax
from jax.experimental import pallas as pl
from jax.experimental.pallas import tpu as pltpu
from jax.sharding import PartitionSpec as P

SPAN = 3
PARTS = 2
LONGEST = 1536


clip_norm = 128.0


def from_behind(block, axis, distance):
    devices = range(lax.axis_size(axis))
    route = [((i - distance) % len(devices), i) for i in devices]
    return lax.ppermute(block, axis, route)


def document_ids(lengths, offset, positions, all_tokens):
    doc_ends = jnp.cumsum(lengths)
    starts = doc_ends - lengths
    longest = jnp.argmax(lengths)
    labels = jnp.arange(lengths.shape[0], dtype=jnp.int32)
    doc_shift = jnp.sum(jnp.where(labels == longest, starts, 0)) + offset
    packed = (positions + doc_shift) % all_tokens
    return jnp.sum((doc_ends[None, :] <= packed[:, None]).astype(jnp.int32), axis=1)


def pair_terms(
    left_ids, left_inner, left_grad, right_ids, right_inner, right_grad, keep_rows, member
):
    inner_gram = jnp.einsum(
        "ir,jr->ij", left_inner, right_inner, preferred_element_type=jnp.float32
    )
    grad_gram = jnp.einsum("id,jd->ij", left_grad, right_grad, preferred_element_type=jnp.float32)
    same_doc = (left_ids[:, None] == right_ids[None, :]) & keep_rows[:, None]
    weight = jnp.sum(jnp.where(same_doc, inner_gram * grad_gram, 0.0), axis=1)
    return jnp.dot(weight, member, precision=lax.Precision.HIGHEST)


def boundary_crossing_plan(
    ids_of, local_document_index, adapter_inner, out_grad, member, my_block, block_rows, all_tokens
):
    first_doc = local_document_index[0]
    last_doc = local_document_index[block_rows - 1]
    before_id = ids_of(jnp.reshape((my_block * block_rows - 1) % all_tokens, (1,)))[0]
    after_id = ids_of(jnp.reshape((my_block + 1) * block_rows % all_tokens, (1,)))[0]
    starts_before = before_id == first_doc
    continues = after_id == last_doc
    crossing = starts_before & (local_document_index == first_doc) | continues & (
        local_document_index == last_doc
    )
    norm_terms = pair_terms(
        local_document_index,
        adapter_inner,
        out_grad,
        local_document_index,
        adapter_inner,
        out_grad,
        jnp.logical_not(crossing),
        member,
    )
    in_first = (local_document_index == first_doc).astype(jnp.bfloat16)
    in_last = (local_document_index == last_doc).astype(jnp.bfloat16)
    first_part = jnp.einsum(
        "tr,td->rd", adapter_inner * in_first[:, None], out_grad, preferred_element_type=jnp.float32
    )
    last_part = jnp.einsum(
        "tr,td->rd", adapter_inner * in_last[:, None], out_grad, preferred_element_type=jnp.float32
    )
    finish = (starts_before & jnp.logical_not((first_doc == last_doc) & continues)).astype(
        jnp.float32
    )
    return (first_doc, last_doc, starts_before, norm_terms, first_part, last_part, finish)


def chain_plan(out_grad, adapter_inner, doc_lengths, slab_offset, included):
    block_rows = out_grad.shape[0]
    ctx_size = lax.axis_size("ctx")
    my_block = lax.axis_index("ctx")
    all_tokens = ctx_size * block_rows
    lengths = doc_lengths[0]
    doc_count = lengths.shape[0]
    row_index = jnp.arange(block_rows, dtype=jnp.int32)
    labels = jnp.arange(doc_count, dtype=jnp.int32)

    def ids_of(positions):
        return document_ids(lengths, slab_offset[0], positions, all_tokens)

    local_document_index = ids_of(my_block * block_rows + row_index)
    member = (local_document_index[:, None] == labels[None, :]).astype(jnp.float32)
    first_doc, last_doc, starts_before, norm_terms, first_part, last_part, finish = (
        boundary_crossing_plan(
            ids_of,
            local_document_index,
            adapter_inner,
            out_grad,
            member,
            my_block,
            block_rows,
            all_tokens,
        )
    )
    chain_flag = (starts_before & (first_doc == last_doc)).astype(jnp.float32)
    running = last_part
    received = jnp.zeros_like(last_part)
    for distance in range(SPAN):
        received = from_behind(running, "ctx", 1)
        running = last_part + chain_flag * received
    complete_document = received + first_part
    end_term = finish * jnp.sum(complete_document * complete_document)
    norm_terms = norm_terms + end_term * (labels == first_doc).astype(jnp.float32)
    squares = lax.psum(norm_terms, "ctx")
    document_grad_norm = jnp.sqrt(squares)
    clip_factor = (
        included[0].astype(jnp.float32) * clip_norm / jnp.maximum(document_grad_norm, clip_norm)
    )
    token_factor = jnp.dot(member, clip_factor, precision=lax.Precision.HIGHEST)
    scaled = (token_factor[:, None] * adapter_inner.astype(jnp.float32)).astype(jnp.bfloat16)
    adapter_second_gradient = lax.psum_scatter(
        jnp.einsum("td,tr->dr", out_grad, scaled, preferred_element_type=jnp.float32),
        ("dp", "ctx"),
        scatter_dimension=0,
        tiled=True,
    )
    return (adapter_second_gradient, document_grad_norm[None, :])


def bits_of(n):
    return n.bit_length() - 1


def halving_orders(n_ctx):
    even = list(range(bits_of(n_ctx)))
    odd = list(even)
    odd[0], odd[1] = odd[1], odd[0]
    return even, odd


def bit_in_use(block, place, n_ctx):
    odd = lax.rem(lax.axis_index("dp"), 2) == 1
    even_order, odd_order = halving_orders(n_ctx)
    return jnp.where(odd, (block >> odd_order[place]) & 1, (block >> even_order[place]) & 1)


def partials_kernel(
    half, n_ctx, docs, chunks, len_hbm, off_hbm, inc_hbm, inner_hbm, grad_hbm, *refs
):
    send_ref, keep_ref, flag_ref, grad_buf, inner_ref, spread = refs[:6]
    len_ref, off_ref, inc_ref, small_sems, sems = refs[6:]
    rank, rows = inner_ref.shape
    features = send_ref.shape[1]
    width = features // chunks
    small = [
        pltpu.make_async_copy(len_hbm, len_ref, small_sems.at[0]),
        pltpu.make_async_copy(off_hbm, off_ref, small_sems.at[1]),
        pltpu.make_async_copy(inner_hbm, inner_ref, small_sems.at[2]),
        pltpu.make_async_copy(inc_hbm, inc_ref, small_sems.at[3]),
    ]
    copies = [
        pltpu.make_async_copy(
            grad_hbm.at[:, pl.ds(half * features + j * width, width)], grad_buf.at[j], sems.at[j]
        )
        for j in range(chunks)
    ]
    for copy in small + copies:
        copy.start()
    for copy in small:
        copy.wait()
    total = n_ctx * rows
    me = lax.axis_index("ctx")
    lengths = [len_ref[0, k] for k in range(docs)]
    starts = [jnp.int32(0)]
    for k in range(1, docs):
        starts.append(starts[-1] + lengths[k - 1])
    longest, best = starts[0], lengths[0]
    for k in range(1, docs):
        better = lengths[k] > best
        longest = jnp.where(better, starts[k], longest)
        best = jnp.where(better, lengths[k], best)
    shift = longest + off_ref[0, 0]
    firsts = []
    for k in range(docs):
        first = starts[k] - shift
        firsts.append(jnp.where(first < 0, first + total, first))
    flip = jnp.int32(0)
    for k in range(docs):
        block = lax.div(firsts[k], jnp.int32(rows))
        offset = firsts[k] - block * rows
        inside = (offset >= 1) & (offset + lengths[k] <= rows - 1)
        flip = flip + jnp.where(inside, ((k + 1) & 1) ^ bit_in_use(block, 0, n_ctx), 0)
    first_bit, second_bit = bit_in_use(me, 0, n_ctx), bit_in_use(me, 1, n_ctx)
    even_order, odd_order = halving_orders(n_ctx)
    odd = lax.rem(lax.axis_index("dp"), 2) == 1
    other = me ^ jnp.where(odd, 1 << odd_order[0], 1 << even_order[0])

    def wrapped(x):
        return jnp.where(x < 0, x + total, x)

    packed = me * rows + shift + lax.broadcasted_iota(jnp.int32, (rank, rows), 1)
    packed = jnp.where(packed >= total, packed - total, packed)
    inner = inner_ref[...].astype(jnp.float32)
    slots = [jnp.zeros_like(inner) for _ in range(3)]
    weights = [jnp.int32(0)] * 2
    flag = jnp.int32(0)
    for k in range(docs):
        mine = ((k & 1) ^ flip) == first_bit
        near = (k >> 1) == second_bit
        belongs = [mine & near, mine & jnp.logical_not(near), jnp.logical_not(mine)]
        inside = (packed >= starts[k]) & (packed < starts[k] + lengths[k])
        rows_of = jnp.where(inside, inner, 0.0)
        for i in range(3):
            slots[i] = slots[i] + jnp.where(belongs[i], 1.0, 0.0) * rows_of
        ahead, behind = firsts[k] - other * rows, other * rows - firsts[k]
        present = (wrapped(ahead) < rows) | (wrapped(behind) < lengths[k])
        for i in range(2):
            weights[i] = weights[i] + jnp.where(belongs[i] & present, 1, 0)
        flag = flag + jnp.where(belongs[0], inc_ref[0, k], 0)
    for i in range(3):
        spread[i * rank : (i + 1) * rank, :] = slots[i].astype(jnp.bfloat16)
    document = 2 * second_bit + (first_bit ^ flip)
    line = lax.broadcasted_iota(jnp.int32, flag_ref.shape, 0)
    facts = jnp.zeros(flag_ref.shape, jnp.float32)
    for i, fact in enumerate([flag, weights[0], weights[1], document]):
        facts = jnp.where(line == i, fact.astype(jnp.float32), facts)
    flag_ref[...] = facts
    left = spread[...]
    for j in range(chunks):
        copies[j].wait()
        product = jnp.dot(left, grad_buf[j], preferred_element_type=jnp.float32)
        columns = slice(j * width, (j + 1) * width)
        keep_ref[0, :, columns] = product[:rank]
        keep_ref[1, :, columns] = product[rank : 2 * rank]
        send_ref[:, columns] = product[2 * rank :]


def fold_kernel(keep_ref, recv_ref, fact_ref, send_ref, left_ref):
    received = recv_ref[...]
    send_ref[...] = keep_ref[1] + fact_ref[2:3, 0:1] * received
    left_ref[...] = keep_ref[0] + fact_ref[1:2, 0:1] * received


def round_kernel(keep_ref, recv_ref, own_ref, mine_ref):
    own = keep_ref[...] + recv_ref[...]
    own_ref[...] = own
    mine_ref[...] = own.astype(jnp.bfloat16)


def swapped(pieces, bit):
    half = len(pieces) // 2
    low, high = pieces[:half], pieces[half:]
    first = [jnp.where(bit == 1, b, a) for a, b in zip(low, high)]
    second = [jnp.where(bit == 1, a, b) for a, b in zip(low, high)]
    return first, second


def relative(pieces, low):
    if len(pieces) == 1:
        return pieces
    first, second = swapped(pieces, (low >> (bits_of(len(pieces)) - 1)) & 1)
    return relative(first, low) + relative(second, low)


def clip_kernel(n_dp, n_ctx, docs, parts, *refs):
    own_refs, mine_refs, other_refs = refs[:parts], refs[parts : 2 * parts], refs[2 * parts : 3 * parts]
    flag_ref, send_ref, keep_ref, norm_ref = refs[3 * parts :]
    slab = send_ref.shape[2]
    span = 2 * slab
    places = n_ctx // 2
    width = slab // places
    square = None
    wholes = []
    for own_ref, mine_ref, other_ref in zip(own_refs, mine_refs, other_refs):
        other = other_ref[...].astype(jnp.float32)
        whole = mine_ref[...].astype(jnp.float32) + other
        wholes.append(own_ref[...] + other)
        term = jnp.sum(whole * whole, keepdims=True)
        square = term if square is None else square + term
    norm = jnp.sqrt(square)
    factor = flag_ref[0:1, 0:1] * clip_norm / jnp.maximum(norm, clip_norm)
    me = lax.axis_index("ctx")
    upper = me // places == 1
    low = lax.rem(me, places)
    dp = lax.axis_index("dp")
    core, chip = lax.rem(dp, 2), dp // 2
    halves = []
    for d in range(n_dp):
        whole = wholes[d * parts // n_dp]
        base = d % (n_dp // parts) * span
        halves.append(
            jnp.where(upper, whole[:, base + slab : base + span], whole[:, base : base + slab])
            * factor
        )
    for target, ref in ((0, keep_ref), (1, send_ref)):
        for x in range(n_dp // 2):
            piece = jnp.where(core == target, halves[2 * x], halves[2 * x + 1])
            pieces = relative([piece[:, q * width : (q + 1) * width] for q in range(places)], low)
            ref[chip ^ x] = jnp.concatenate(pieces, axis=1)
    rows = lax.broadcasted_iota(jnp.int32, norm_ref.shape, 0).astype(jnp.float32)
    norm_ref[...] = jnp.where(rows == flag_ref[3:4, :], norm, 0.0)


def core_kernel(keep_ref, recv_ref, send_ref):
    send_ref[...] = keep_ref[1] + recv_ref[1]


def with_norms(block, norms, send_ref):
    width = block.shape[1]
    spare = send_ref.shape[1] - width
    send_ref[...] = jnp.concatenate([block, norms[:, :spare]], axis=1)


def chip_kernel(keep_ref, core_ref, recv_ref, norm_ref, send_ref, left_ref):
    total = keep_ref[0] + core_ref[0] + recv_ref[...]
    half = total.shape[1] // 2
    left_ref[...] = total[:, :half]
    with_norms(total[:, half:], norm_ref[...], send_ref)


def step_kernel(keep_ref, recv_ref, norm_ref, send_ref, left_ref, norms_ref):
    width = keep_ref.shape[1]
    half = width // 2
    received = recv_ref[...]
    total = keep_ref[...] + received[:, :width]
    norms = norm_ref[...] + received[:, width : width + 1]
    left_ref[...] = total[:, :half]
    norms_ref[...] = norms
    with_norms(total[:, half:], norms, send_ref)


def last_kernel(docs, keep_ref, recv_ref, norm_ref, out_ref, norms_ref):
    width = keep_ref.shape[1]
    received = recv_ref[...]
    out_ref[...] = keep_ref[...] + received[:, :width]
    norms = norm_ref[...] + received[:, width : width + 1]
    rows = lax.broadcasted_iota(jnp.int32, norms.shape, 0)
    lanes = lax.broadcasted_iota(jnp.int32, norms.shape, 1)
    norms_ref[...] = jnp.sum(jnp.where(rows == lanes, norms, 0.0), axis=0, keepdims=True)[:, :docs]


def exchange(block, n_dp, n_ctx, even_bit, odd_bit):
    route = [
        (d * n_ctx + c, d * n_ctx + (c ^ (1 << (odd_bit if d % 2 else even_bit))))
        for d in range(n_dp)
        for c in range(n_ctx)
    ]
    return lax.ppermute(block, ("dp", "ctx"), route)


def swap_dp(block, n_dp, bit):
    return lax.ppermute(block, "dp", [(d, d ^ (1 << bit)) for d in range(n_dp)])


def in_vmem(kernel, shapes, *operands, scalars=()):
    vmem = pl.BlockSpec(memory_space=pltpu.VMEM)
    smem = pl.BlockSpec(memory_space=pltpu.SMEM)
    return pl.pallas_call(
        kernel,
        out_shape=[pltpu.VMEM(shape, dtype) for shape, dtype in shapes],
        in_specs=[smem] * len(scalars) + [vmem] * len(operands),
        out_specs=[vmem] * len(shapes),
    )(*scalars, *[pltpu.with_memory_space_constraint(x, pltpu.VMEM) for x in operands])


def halving_plan(out_grad, adapter_inner, doc_lengths, slab_offset, included):
    n_dp, n_ctx = lax.axis_size("dp"), lax.axis_size("ctx")
    rows, features = out_grad.shape
    rank = adapter_inner.shape[1]
    docs = doc_lengths.shape[1]
    f32 = jnp.float32
    vmem = pl.BlockSpec(memory_space=pltpu.VMEM)
    hbm = pl.BlockSpec(memory_space=pl.ANY)
    parts = PARTS
    part = features // parts
    chunks = max(1, part // 768)
    column = ((rank, 128), f32)
    single = ((rank, part), f32)

    def partials(half):
        return pl.pallas_call(
            functools.partial(partials_kernel, half, n_ctx, docs, chunks),
            out_shape=[
                pltpu.VMEM(*single),
                pltpu.VMEM((2, rank, part), f32),
                pltpu.VMEM((8, 128), f32),
            ],
            in_specs=[hbm] * 5,
            out_specs=[vmem] * 3,
            scratch_shapes=[
                pltpu.VMEM((chunks, rows, part // chunks), jnp.bfloat16),
                pltpu.VMEM((rank, rows), jnp.bfloat16),
                pltpu.VMEM((3 * rank, rows), jnp.bfloat16),
                pltpu.SMEM(doc_lengths.shape, jnp.int32),
                pltpu.SMEM((1, 1), jnp.int32),
                pltpu.SMEM(included.shape, jnp.int32),
                pltpu.SemaphoreType.DMA((4,)),
                pltpu.SemaphoreType.DMA((chunks,)),
            ],
            cost_estimate=pl.CostEstimate(
                flops=2 * 3 * rank * rows * part,
                bytes_accessed=2 * rows * part,
                transcendentals=0,
            ),
        )(doc_lengths, slab_offset[:, None], included, adapter_inner.T, out_grad)

    even, odd = halving_orders(n_ctx)
    rounds = list(zip(even, odd))
    owns, mines, others = [], [], []
    for half in range(parts):
        send, keep, flag = partials(half)
        received = exchange(send, n_dp, n_ctx, *rounds[0])
        send, keep = in_vmem(fold_kernel, [single, single], keep, received, flag)
        received = exchange(send, n_dp, n_ctx, *rounds[1])
        own, mine = in_vmem(
            round_kernel, [single, ((rank, part), jnp.bfloat16)], keep, received
        )
        owns.append(own)
        mines.append(mine)
        others.append(exchange(mine, n_dp, n_ctx, *rounds[-1]))
    slab = features // (2 * n_dp)
    pieces = ((n_dp // 2, rank, slab), f32)
    send, keep, norms = in_vmem(
        functools.partial(clip_kernel, n_dp, n_ctx, docs, parts),
        [pieces, pieces, column],
        *owns,
        *mines,
        *others,
        flag,
    )
    core = swap_dp(send, n_dp, 0)
    (send,) = in_vmem(core_kernel, [((rank, slab), f32)], keep, core)
    received = swap_dp(send, n_dp, 1)

    def shapes(width):
        return [((rank, width // 128 * 128 + 128), f32), ((rank, width), f32)]

    width = slab // 2
    steps = list(reversed(range(bits_of(n_ctx // 2))))
    send, keep = in_vmem(chip_kernel, shapes(width), keep, core, received, norms)
    for bit in steps[:-1]:
        width //= 2
        received = exchange(send, n_dp, n_ctx, bit, bit)
        send, keep, norms = in_vmem(step_kernel, shapes(width) + [column], keep, received, norms)
    received = exchange(send, n_dp, n_ctx, steps[-1], steps[-1])
    result, norms = pl.pallas_call(
        functools.partial(last_kernel, docs),
        out_shape=[
            jax.ShapeDtypeStruct((rank, width), f32),
            jax.ShapeDtypeStruct((1, docs), f32),
        ],
        in_specs=[vmem] * 3,
        out_specs=[vmem, vmem],
    )(*[pltpu.with_memory_space_constraint(x, pltpu.VMEM) for x in (keep, received, norms)])
    return (result.T, norms)


def on_device(out_grad, adapter_inner, doc_lengths, slab_offset, included):
    n_dp, n_ctx = lax.axis_size("dp"), lax.axis_size("ctx")
    docs = doc_lengths.shape[1]
    rows = out_grad.shape[0]
    halving = (
        n_dp == 4
        and docs == 4
        and n_ctx == 2 * docs
        and docs <= adapter_inner.shape[1]
        and 2 * (rows - 2) + (docs - 2) * LONGEST < n_ctx * rows
        and out_grad.shape[1] % (768 * PARTS) == 0
    )
    plan = halving_plan if halving else chain_plan
    return plan(out_grad, adapter_inner, doc_lengths, slab_offset, included)


def solution(mesh):
    placed = (P(("dp", "ctx"), None), P(("dp", "ctx"), None), P("dp", None), P("dp"), P("dp", None))
    return jax.shard_map(
        on_device,
        mesh=mesh,
        in_specs=placed,
        out_specs=(P(("dp", "ctx"), None), P("dp", None)),
        check_vma=False,
    )
```

```python
import functools

import jax
import jax.numpy as jnp
from jax import lax
from jax.experimental import pallas as pl
from jax.experimental.pallas import tpu as pltpu
from jax.sharding import PartitionSpec as P

SPAN = 3
PARTS = 2
LONGEST = 1536


clip_norm = 128.0


def from_behind(block, axis, distance):
    devices = range(lax.axis_size(axis))
    route = [((i - distance) % len(devices), i) for i in devices]
    return lax.ppermute(block, axis, route)


def document_ids(lengths, offset, positions, all_tokens):
    doc_ends = jnp.cumsum(lengths)
    starts = doc_ends - lengths
    longest = jnp.argmax(lengths)
    labels = jnp.arange(lengths.shape[0], dtype=jnp.int32)
    doc_shift = jnp.sum(jnp.where(labels == longest, starts, 0)) + offset
    packed = (positions + doc_shift) % all_tokens
    return jnp.sum((doc_ends[None, :] <= packed[:, None]).astype(jnp.int32), axis=1)


def pair_terms(
    left_ids, left_inner, left_grad, right_ids, right_inner, right_grad, keep_rows, member
):
    inner_gram = jnp.einsum(
        "ir,jr->ij", left_inner, right_inner, preferred_element_type=jnp.float32
    )
    grad_gram = jnp.einsum("id,jd->ij", left_grad, right_grad, preferred_element_type=jnp.float32)
    same_doc = (left_ids[:, None] == right_ids[None, :]) & keep_rows[:, None]
    weight = jnp.sum(jnp.where(same_doc, inner_gram * grad_gram, 0.0), axis=1)
    return jnp.dot(weight, member, precision=lax.Precision.HIGHEST)


def boundary_crossing_plan(
    ids_of, local_document_index, adapter_inner, out_grad, member, my_block, block_rows, all_tokens
):
    first_doc = local_document_index[0]
    last_doc = local_document_index[block_rows - 1]
    before_id = ids_of(jnp.reshape((my_block * block_rows - 1) % all_tokens, (1,)))[0]
    after_id = ids_of(jnp.reshape((my_block + 1) * block_rows % all_tokens, (1,)))[0]
    starts_before = before_id == first_doc
    continues = after_id == last_doc
    crossing = starts_before & (local_document_index == first_doc) | continues & (
        local_document_index == last_doc
    )
    norm_terms = pair_terms(
        local_document_index,
        adapter_inner,
        out_grad,
        local_document_index,
        adapter_inner,
        out_grad,
        jnp.logical_not(crossing),
        member,
    )
    in_first = (local_document_index == first_doc).astype(jnp.bfloat16)
    in_last = (local_document_index == last_doc).astype(jnp.bfloat16)
    first_part = jnp.einsum(
        "tr,td->rd", adapter_inner * in_first[:, None], out_grad, preferred_element_type=jnp.float32
    )
    last_part = jnp.einsum(
        "tr,td->rd", adapter_inner * in_last[:, None], out_grad, preferred_element_type=jnp.float32
    )
    finish = (starts_before & jnp.logical_not((first_doc == last_doc) & continues)).astype(
        jnp.float32
    )
    return (first_doc, last_doc, starts_before, norm_terms, first_part, last_part, finish)


def chain_plan(out_grad, adapter_inner, doc_lengths, slab_offset, included):
    block_rows = out_grad.shape[0]
    ctx_size = lax.axis_size("ctx")
    my_block = lax.axis_index("ctx")
    all_tokens = ctx_size * block_rows
    lengths = doc_lengths[0]
    doc_count = lengths.shape[0]
    row_index = jnp.arange(block_rows, dtype=jnp.int32)
    labels = jnp.arange(doc_count, dtype=jnp.int32)

    def ids_of(positions):
        return document_ids(lengths, slab_offset[0], positions, all_tokens)

    local_document_index = ids_of(my_block * block_rows + row_index)
    member = (local_document_index[:, None] == labels[None, :]).astype(jnp.float32)
    first_doc, last_doc, starts_before, norm_terms, first_part, last_part, finish = (
        boundary_crossing_plan(
            ids_of,
            local_document_index,
            adapter_inner,
            out_grad,
            member,
            my_block,
            block_rows,
            all_tokens,
        )
    )
    chain_flag = (starts_before & (first_doc == last_doc)).astype(jnp.float32)
    running = last_part
    received = jnp.zeros_like(last_part)
    for distance in range(SPAN):
        received = from_behind(running, "ctx", 1)
        running = last_part + chain_flag * received
    complete_document = received + first_part
    end_term = finish * jnp.sum(complete_document * complete_document)
    norm_terms = norm_terms + end_term * (labels == first_doc).astype(jnp.float32)
    squares = lax.psum(norm_terms, "ctx")
    document_grad_norm = jnp.sqrt(squares)
    clip_factor = (
        included[0].astype(jnp.float32) * clip_norm / jnp.maximum(document_grad_norm, clip_norm)
    )
    token_factor = jnp.dot(member, clip_factor, precision=lax.Precision.HIGHEST)
    scaled = (token_factor[:, None] * adapter_inner.astype(jnp.float32)).astype(jnp.bfloat16)
    adapter_second_gradient = lax.psum_scatter(
        jnp.einsum("td,tr->dr", out_grad, scaled, preferred_element_type=jnp.float32),
        ("dp", "ctx"),
        scatter_dimension=0,
        tiled=True,
    )
    return (adapter_second_gradient, document_grad_norm[None, :])


def bits_of(n):
    return n.bit_length() - 1


def halving_orders(n_ctx):
    even = list(range(bits_of(n_ctx)))
    odd = list(even)
    odd[0], odd[1] = odd[1], odd[0]
    return even, odd


def bit_in_use(block, place, n_ctx):
    odd = lax.rem(lax.axis_index("dp"), 2) == 1
    even_order, odd_order = halving_orders(n_ctx)
    return jnp.where(odd, (block >> odd_order[place]) & 1, (block >> even_order[place]) & 1)


def partials_kernel(
    n_ctx, docs, chunks, len_hbm, off_hbm, inc_hbm, inner_hbm, grad_hbm, *refs
):
    send_refs, (keep_ref, flag_ref, grad_buf, inner_ref, spread) = refs[:PARTS], refs[PARTS : PARTS + 5]
    len_ref, off_ref, inc_ref, small_sems, sems = refs[PARTS + 5 :]
    rank, rows = inner_ref.shape
    part = send_refs[0].shape[1]
    width = grad_hbm.shape[1] // chunks
    small = [
        pltpu.make_async_copy(len_hbm, len_ref, small_sems.at[0]),
        pltpu.make_async_copy(off_hbm, off_ref, small_sems.at[1]),
        pltpu.make_async_copy(inner_hbm, inner_ref, small_sems.at[2]),
        pltpu.make_async_copy(inc_hbm, inc_ref, small_sems.at[3]),
    ]
    copies = [
        pltpu.make_async_copy(
            grad_hbm.at[:, pl.ds(j * width, width)], grad_buf.at[j], sems.at[j]
        )
        for j in range(chunks)
    ]
    for copy in small + copies:
        copy.start()
    for copy in small:
        copy.wait()
    total = n_ctx * rows
    me = lax.axis_index("ctx")
    lengths = [len_ref[0, k] for k in range(docs)]
    starts = [jnp.int32(0)]
    for k in range(1, docs):
        starts.append(starts[-1] + lengths[k - 1])
    longest, best = starts[0], lengths[0]
    for k in range(1, docs):
        better = lengths[k] > best
        longest = jnp.where(better, starts[k], longest)
        best = jnp.where(better, lengths[k], best)
    shift = longest + off_ref[0, 0]
    firsts = []
    for k in range(docs):
        first = starts[k] - shift
        firsts.append(jnp.where(first < 0, first + total, first))
    flip = jnp.int32(0)
    for k in range(docs):
        block = lax.div(firsts[k], jnp.int32(rows))
        offset = firsts[k] - block * rows
        inside = (offset >= 1) & (offset + lengths[k] <= rows - 1)
        flip = flip + jnp.where(inside, ((k + 1) & 1) ^ bit_in_use(block, 0, n_ctx), 0)
    first_bit, second_bit = bit_in_use(me, 0, n_ctx), bit_in_use(me, 1, n_ctx)
    even_order, odd_order = halving_orders(n_ctx)
    odd = lax.rem(lax.axis_index("dp"), 2) == 1
    other = me ^ jnp.where(odd, 1 << odd_order[0], 1 << even_order[0])

    def wrapped(x):
        return jnp.where(x < 0, x + total, x)

    packed = me * rows + shift + lax.broadcasted_iota(jnp.int32, (rank, rows), 1)
    packed = jnp.where(packed >= total, packed - total, packed)
    inner = inner_ref[...].astype(jnp.float32)
    slots = [jnp.zeros_like(inner) for _ in range(3)]
    weights = [jnp.int32(0)] * 2
    flag = jnp.int32(0)
    for k in range(docs):
        mine = ((k & 1) ^ flip) == first_bit
        near = (k >> 1) == second_bit
        belongs = [mine & near, mine & jnp.logical_not(near), jnp.logical_not(mine)]
        inside = (packed >= starts[k]) & (packed < starts[k] + lengths[k])
        rows_of = jnp.where(inside, inner, 0.0)
        for i in range(3):
            slots[i] = slots[i] + jnp.where(belongs[i], 1.0, 0.0) * rows_of
        ahead, behind = firsts[k] - other * rows, other * rows - firsts[k]
        present = (wrapped(ahead) < rows) | (wrapped(behind) < lengths[k])
        for i in range(2):
            weights[i] = weights[i] + jnp.where(belongs[i] & present, 1, 0)
        flag = flag + jnp.where(belongs[0], inc_ref[0, k], 0)
    for i in range(3):
        spread[i * rank : (i + 1) * rank, :] = slots[i].astype(jnp.bfloat16)
    document = 2 * second_bit + (first_bit ^ flip)
    line = lax.broadcasted_iota(jnp.int32, flag_ref.shape, 0)
    facts = jnp.zeros(flag_ref.shape, jnp.float32)
    for i, fact in enumerate([flag, weights[0], weights[1], document]):
        facts = jnp.where(line == i, fact.astype(jnp.float32), facts)
    flag_ref[...] = facts
    left = spread[...]
    for j in range(chunks):
        copies[j].wait()
        product = jnp.dot(left, grad_buf[j], preferred_element_type=jnp.float32)
        columns = slice(j * width, (j + 1) * width)
        keep_ref[0, :, columns] = product[:rank]
        keep_ref[1, :, columns] = product[rank : 2 * rank]
        at = j * width % part
        send_refs[j * width // part][:, at : at + width] = product[2 * rank :]


def fold_kernel(half, keep_ref, recv_ref, fact_ref, send_ref, left_ref):
    width = send_ref.shape[1]
    columns = slice(half * width, (half + 1) * width)
    received = recv_ref[...]
    send_ref[...] = keep_ref[1, :, columns] + fact_ref[2:3, 0:1] * received
    left_ref[...] = keep_ref[0, :, columns] + fact_ref[1:2, 0:1] * received


def round_kernel(keep_ref, recv_ref, own_ref, mine_ref):
    own = keep_ref[...] + recv_ref[...]
    own_ref[...] = own
    mine_ref[...] = own.astype(jnp.bfloat16)


def swapped(pieces, bit):
    half = len(pieces) // 2
    low, high = pieces[:half], pieces[half:]
    first = [jnp.where(bit == 1, b, a) for a, b in zip(low, high)]
    second = [jnp.where(bit == 1, a, b) for a, b in zip(low, high)]
    return first, second


def relative(pieces, low):
    if len(pieces) == 1:
        return pieces
    first, second = swapped(pieces, (low >> (bits_of(len(pieces)) - 1)) & 1)
    return relative(first, low) + relative(second, low)


def clip_kernel(n_dp, n_ctx, docs, parts, *refs):
    own_refs, mine_refs, other_refs = refs[:parts], refs[parts : 2 * parts], refs[2 * parts : 3 * parts]
    flag_ref, send_ref, keep_ref, norm_ref = refs[3 * parts :]
    slab = send_ref.shape[2]
    span = 2 * slab
    places = n_ctx // 2
    width = slab // places
    square = None
    wholes = []
    for own_ref, mine_ref, other_ref in zip(own_refs, mine_refs, other_refs):
        other = other_ref[...].astype(jnp.float32)
        whole = mine_ref[...].astype(jnp.float32) + other
        wholes.append(own_ref[...] + other)
        term = jnp.sum(whole * whole, keepdims=True)
        square = term if square is None else square + term
    norm = jnp.sqrt(square)
    factor = flag_ref[0:1, 0:1] * clip_norm / jnp.maximum(norm, clip_norm)
    me = lax.axis_index("ctx")
    upper = me // places == 1
    low = lax.rem(me, places)
    dp = lax.axis_index("dp")
    core, chip = lax.rem(dp, 2), dp // 2
    halves = []
    for d in range(n_dp):
        whole = wholes[d * parts // n_dp]
        base = d % (n_dp // parts) * span
        halves.append(
            jnp.where(upper, whole[:, base + slab : base + span], whole[:, base : base + slab])
            * factor
        )
    for target, ref in ((0, keep_ref), (1, send_ref)):
        for x in range(n_dp // 2):
            piece = jnp.where(core == target, halves[2 * x], halves[2 * x + 1])
            pieces = relative([piece[:, q * width : (q + 1) * width] for q in range(places)], low)
            ref[chip ^ x] = jnp.concatenate(pieces, axis=1)
    rows = lax.broadcasted_iota(jnp.int32, norm_ref.shape, 0).astype(jnp.float32)
    norm_ref[...] = jnp.where(rows == flag_ref[3:4, :], norm, 0.0)


def core_kernel(keep_ref, recv_ref, send_ref):
    send_ref[...] = keep_ref[1] + recv_ref[1]


def with_norms(block, norms, send_ref):
    width = block.shape[1]
    spare = send_ref.shape[1] - width
    send_ref[...] = jnp.concatenate([block, norms[:, :spare]], axis=1)


def chip_kernel(keep_ref, core_ref, recv_ref, norm_ref, send_ref, left_ref):
    total = keep_ref[0] + core_ref[0] + recv_ref[...]
    half = total.shape[1] // 2
    left_ref[...] = total[:, :half]
    with_norms(total[:, half:], norm_ref[...], send_ref)


def step_kernel(keep_ref, recv_ref, norm_ref, send_ref, left_ref, norms_ref):
    width = keep_ref.shape[1]
    half = width // 2
    received = recv_ref[...]
    total = keep_ref[...] + received[:, :width]
    norms = norm_ref[...] + received[:, width : width + 1]
    left_ref[...] = total[:, :half]
    norms_ref[...] = norms
    with_norms(total[:, half:], norms, send_ref)


def last_kernel(docs, keep_ref, recv_ref, norm_ref, out_ref, norms_ref):
    width = keep_ref.shape[1]
    received = recv_ref[...]
    out_ref[...] = keep_ref[...] + received[:, :width]
    norms = norm_ref[...] + received[:, width : width + 1]
    rows = lax.broadcasted_iota(jnp.int32, norms.shape, 0)
    lanes = lax.broadcasted_iota(jnp.int32, norms.shape, 1)
    norms_ref[...] = jnp.sum(jnp.where(rows == lanes, norms, 0.0), axis=0, keepdims=True)[:, :docs]


def exchange(block, n_dp, n_ctx, even_bit, odd_bit):
    route = [
        (d * n_ctx + c, d * n_ctx + (c ^ (1 << (odd_bit if d % 2 else even_bit))))
        for d in range(n_dp)
        for c in range(n_ctx)
    ]
    return lax.ppermute(block, ("dp", "ctx"), route)


def swap_dp(block, n_dp, bit):
    return lax.ppermute(block, "dp", [(d, d ^ (1 << bit)) for d in range(n_dp)])


def in_vmem(kernel, shapes, *operands, scalars=()):
    vmem = pl.BlockSpec(memory_space=pltpu.VMEM)
    smem = pl.BlockSpec(memory_space=pltpu.SMEM)
    return pl.pallas_call(
        kernel,
        out_shape=[pltpu.VMEM(shape, dtype) for shape, dtype in shapes],
        in_specs=[smem] * len(scalars) + [vmem] * len(operands),
        out_specs=[vmem] * len(shapes),
    )(*scalars, *[pltpu.with_memory_space_constraint(x, pltpu.VMEM) for x in operands])


def halving_plan(out_grad, adapter_inner, doc_lengths, slab_offset, included):
    n_dp, n_ctx = lax.axis_size("dp"), lax.axis_size("ctx")
    rows, features = out_grad.shape
    rank = adapter_inner.shape[1]
    docs = doc_lengths.shape[1]
    f32 = jnp.float32
    vmem = pl.BlockSpec(memory_space=pltpu.VMEM)
    hbm = pl.BlockSpec(memory_space=pl.ANY)
    parts = PARTS
    part = features // parts
    chunks = max(1, features // 1152)
    column = ((rank, 128), f32)
    single = ((rank, part), f32)

    *sends, keep, flag = pl.pallas_call(
        functools.partial(partials_kernel, n_ctx, docs, chunks),
        out_shape=[
            *[pltpu.VMEM(*single)] * parts,
            pltpu.VMEM((2, rank, features), f32),
            pltpu.VMEM((8, 128), f32),
        ],
        in_specs=[hbm] * 5,
        out_specs=[vmem] * (parts + 2),
        scratch_shapes=[
            pltpu.VMEM((chunks, rows, features // chunks), jnp.bfloat16),
            pltpu.VMEM((rank, rows), jnp.bfloat16),
            pltpu.VMEM((3 * rank, rows), jnp.bfloat16),
            pltpu.SMEM(doc_lengths.shape, jnp.int32),
            pltpu.SMEM((1, 1), jnp.int32),
            pltpu.SMEM(included.shape, jnp.int32),
            pltpu.SemaphoreType.DMA((4,)),
            pltpu.SemaphoreType.DMA((chunks,)),
        ],
        cost_estimate=pl.CostEstimate(
            flops=2 * 3 * rank * rows * features,
            bytes_accessed=2 * rows * features,
            transcendentals=0,
        ),
    )(doc_lengths, slab_offset[:, None], included, adapter_inner.T, out_grad)

    even, odd = halving_orders(n_ctx)
    rounds = list(zip(even, odd))
    owns, mines, others = [], [], []
    firsts = [exchange(send, n_dp, n_ctx, *rounds[0]) for send in sends]
    for half in range(parts):
        send, left = in_vmem(
            functools.partial(fold_kernel, half), [single, single], keep, firsts[half], flag
        )
        received = exchange(send, n_dp, n_ctx, *rounds[1])
        own, mine = in_vmem(
            round_kernel, [single, ((rank, part), jnp.bfloat16)], left, received
        )
        owns.append(own)
        mines.append(mine)
        others.append(exchange(mine, n_dp, n_ctx, *rounds[-1]))
    slab = features // (2 * n_dp)
    pieces = ((n_dp // 2, rank, slab), f32)
    send, keep, norms = in_vmem(
        functools.partial(clip_kernel, n_dp, n_ctx, docs, parts),
        [pieces, pieces, column],
        *owns,
        *mines,
        *others,
        flag,
    )
    core = swap_dp(send, n_dp, 0)
    (send,) = in_vmem(core_kernel, [((rank, slab), f32)], keep, core)
    received = swap_dp(send, n_dp, 1)

    def shapes(width):
        return [((rank, width // 128 * 128 + 128), f32), ((rank, width), f32)]

    width = slab // 2
    steps = list(reversed(range(bits_of(n_ctx // 2))))
    send, keep = in_vmem(chip_kernel, shapes(width), keep, core, received, norms)
    for bit in steps[:-1]:
        width //= 2
        received = exchange(send, n_dp, n_ctx, bit, bit)
        send, keep, norms = in_vmem(step_kernel, shapes(width) + [column], keep, received, norms)
    received = exchange(send, n_dp, n_ctx, steps[-1], steps[-1])
    result, norms = pl.pallas_call(
        functools.partial(last_kernel, docs),
        out_shape=[
            jax.ShapeDtypeStruct((rank, width), f32),
            jax.ShapeDtypeStruct((1, docs), f32),
        ],
        in_specs=[vmem] * 3,
        out_specs=[vmem, vmem],
    )(*[pltpu.with_memory_space_constraint(x, pltpu.VMEM) for x in (keep, received, norms)])
    return (result.T, norms)


def on_device(out_grad, adapter_inner, doc_lengths, slab_offset, included):
    n_dp, n_ctx = lax.axis_size("dp"), lax.axis_size("ctx")
    docs = doc_lengths.shape[1]
    rows = out_grad.shape[0]
    halving = (
        n_dp == 4
        and docs == 4
        and n_ctx == 2 * docs
        and docs <= adapter_inner.shape[1]
        and 2 * (rows - 2) + (docs - 2) * LONGEST < n_ctx * rows
        and out_grad.shape[1] % (1152 * PARTS) == 0
    )
    plan = halving_plan if halving else chain_plan
    return plan(out_grad, adapter_inner, doc_lengths, slab_offset, included)


def solution(mesh):
    placed = (P(("dp", "ctx"), None), P(("dp", "ctx"), None), P("dp", None), P("dp"), P("dp", None))
    return jax.shard_map(
        on_device,
        mesh=mesh,
        in_specs=placed,
        out_specs=(P(("dp", "ctx"), None), P("dp", None)),
        check_vma=False,
    )
```

```python
import functools

import jax
import jax.numpy as jnp
from jax import lax
from jax.experimental import pallas as pl
from jax.experimental.pallas import tpu as pltpu
from jax.sharding import PartitionSpec as P

SPAN = 3
PARTS = 2
LONGEST = 1536


clip_norm = 128.0


def from_behind(block, axis, distance):
    devices = range(lax.axis_size(axis))
    route = [((i - distance) % len(devices), i) for i in devices]
    return lax.ppermute(block, axis, route)


def document_ids(lengths, offset, positions, all_tokens):
    doc_ends = jnp.cumsum(lengths)
    starts = doc_ends - lengths
    longest = jnp.argmax(lengths)
    labels = jnp.arange(lengths.shape[0], dtype=jnp.int32)
    doc_shift = jnp.sum(jnp.where(labels == longest, starts, 0)) + offset
    packed = (positions + doc_shift) % all_tokens
    return jnp.sum((doc_ends[None, :] <= packed[:, None]).astype(jnp.int32), axis=1)


def pair_terms(
    left_ids, left_inner, left_grad, right_ids, right_inner, right_grad, keep_rows, member
):
    inner_gram = jnp.einsum(
        "ir,jr->ij", left_inner, right_inner, preferred_element_type=jnp.float32
    )
    grad_gram = jnp.einsum("id,jd->ij", left_grad, right_grad, preferred_element_type=jnp.float32)
    same_doc = (left_ids[:, None] == right_ids[None, :]) & keep_rows[:, None]
    weight = jnp.sum(jnp.where(same_doc, inner_gram * grad_gram, 0.0), axis=1)
    return jnp.dot(weight, member, precision=lax.Precision.HIGHEST)


def boundary_crossing_plan(
    ids_of, local_document_index, adapter_inner, out_grad, member, my_block, block_rows, all_tokens
):
    first_doc = local_document_index[0]
    last_doc = local_document_index[block_rows - 1]
    before_id = ids_of(jnp.reshape((my_block * block_rows - 1) % all_tokens, (1,)))[0]
    after_id = ids_of(jnp.reshape((my_block + 1) * block_rows % all_tokens, (1,)))[0]
    starts_before = before_id == first_doc
    continues = after_id == last_doc
    crossing = starts_before & (local_document_index == first_doc) | continues & (
        local_document_index == last_doc
    )
    norm_terms = pair_terms(
        local_document_index,
        adapter_inner,
        out_grad,
        local_document_index,
        adapter_inner,
        out_grad,
        jnp.logical_not(crossing),
        member,
    )
    in_first = (local_document_index == first_doc).astype(jnp.bfloat16)
    in_last = (local_document_index == last_doc).astype(jnp.bfloat16)
    first_part = jnp.einsum(
        "tr,td->rd", adapter_inner * in_first[:, None], out_grad, preferred_element_type=jnp.float32
    )
    last_part = jnp.einsum(
        "tr,td->rd", adapter_inner * in_last[:, None], out_grad, preferred_element_type=jnp.float32
    )
    finish = (starts_before & jnp.logical_not((first_doc == last_doc) & continues)).astype(
        jnp.float32
    )
    return (first_doc, last_doc, starts_before, norm_terms, first_part, last_part, finish)


def chain_plan(out_grad, adapter_inner, doc_lengths, slab_offset, included):
    block_rows = out_grad.shape[0]
    ctx_size = lax.axis_size("ctx")
    my_block = lax.axis_index("ctx")
    all_tokens = ctx_size * block_rows
    lengths = doc_lengths[0]
    doc_count = lengths.shape[0]
    row_index = jnp.arange(block_rows, dtype=jnp.int32)
    labels = jnp.arange(doc_count, dtype=jnp.int32)

    def ids_of(positions):
        return document_ids(lengths, slab_offset[0], positions, all_tokens)

    local_document_index = ids_of(my_block * block_rows + row_index)
    member = (local_document_index[:, None] == labels[None, :]).astype(jnp.float32)
    first_doc, last_doc, starts_before, norm_terms, first_part, last_part, finish = (
        boundary_crossing_plan(
            ids_of,
            local_document_index,
            adapter_inner,
            out_grad,
            member,
            my_block,
            block_rows,
            all_tokens,
        )
    )
    chain_flag = (starts_before & (first_doc == last_doc)).astype(jnp.float32)
    running = last_part
    received = jnp.zeros_like(last_part)
    for distance in range(SPAN):
        received = from_behind(running, "ctx", 1)
        running = last_part + chain_flag * received
    complete_document = received + first_part
    end_term = finish * jnp.sum(complete_document * complete_document)
    norm_terms = norm_terms + end_term * (labels == first_doc).astype(jnp.float32)
    squares = lax.psum(norm_terms, "ctx")
    document_grad_norm = jnp.sqrt(squares)
    clip_factor = (
        included[0].astype(jnp.float32) * clip_norm / jnp.maximum(document_grad_norm, clip_norm)
    )
    token_factor = jnp.dot(member, clip_factor, precision=lax.Precision.HIGHEST)
    scaled = (token_factor[:, None] * adapter_inner.astype(jnp.float32)).astype(jnp.bfloat16)
    adapter_second_gradient = lax.psum_scatter(
        jnp.einsum("td,tr->dr", out_grad, scaled, preferred_element_type=jnp.float32),
        ("dp", "ctx"),
        scatter_dimension=0,
        tiled=True,
    )
    return (adapter_second_gradient, document_grad_norm[None, :])


def bits_of(n):
    return n.bit_length() - 1


def halving_orders(n_ctx):
    even = list(range(bits_of(n_ctx)))
    odd = list(even)
    odd[0], odd[1] = odd[1], odd[0]
    return even, odd


def bit_in_use(block, place, n_ctx):
    odd = lax.rem(lax.axis_index("dp"), 2) == 1
    even_order, odd_order = halving_orders(n_ctx)
    return jnp.where(odd, (block >> odd_order[place]) & 1, (block >> even_order[place]) & 1)


def partials_kernel(
    n_ctx, docs, chunks, len_hbm, off_hbm, inc_hbm, inner_hbm, grad_hbm, *refs
):
    send_refs, (keep_ref, flag_ref, grad_buf, inner_ref, spread) = refs[:PARTS], refs[PARTS : PARTS + 5]
    len_ref, off_ref, inc_ref, small_sems, sems = refs[PARTS + 5 :]
    rank, rows = inner_ref.shape
    part = send_refs[0].shape[1]
    width = grad_hbm.shape[1] // chunks
    small = [
        pltpu.make_async_copy(len_hbm, len_ref, small_sems.at[0]),
        pltpu.make_async_copy(off_hbm, off_ref, small_sems.at[1]),
        pltpu.make_async_copy(inner_hbm, inner_ref, small_sems.at[2]),
        pltpu.make_async_copy(inc_hbm, inc_ref, small_sems.at[3]),
    ]
    copies = [
        pltpu.make_async_copy(
            grad_hbm.at[:, pl.ds(j * width, width)], grad_buf.at[j], sems.at[j]
        )
        for j in range(chunks)
    ]
    for copy in small + copies:
        copy.start()
    for copy in small:
        copy.wait()
    total = n_ctx * rows
    me = lax.axis_index("ctx")
    lengths = [len_ref[0, k] for k in range(docs)]
    starts = [jnp.int32(0)]
    for k in range(1, docs):
        starts.append(starts[-1] + lengths[k - 1])
    longest, best = starts[0], lengths[0]
    for k in range(1, docs):
        better = lengths[k] > best
        longest = jnp.where(better, starts[k], longest)
        best = jnp.where(better, lengths[k], best)
    shift = longest + off_ref[0, 0]
    firsts = []
    for k in range(docs):
        first = starts[k] - shift
        firsts.append(jnp.where(first < 0, first + total, first))
    flip = jnp.int32(0)
    for k in range(docs):
        block = lax.div(firsts[k], jnp.int32(rows))
        offset = firsts[k] - block * rows
        inside = (offset >= 1) & (offset + lengths[k] <= rows - 1)
        flip = flip + jnp.where(inside, ((k + 1) & 1) ^ bit_in_use(block, 0, n_ctx), 0)
    first_bit, second_bit = bit_in_use(me, 0, n_ctx), bit_in_use(me, 1, n_ctx)
    even_order, odd_order = halving_orders(n_ctx)
    odd = lax.rem(lax.axis_index("dp"), 2) == 1
    other = me ^ jnp.where(odd, 1 << odd_order[0], 1 << even_order[0])

    def wrapped(x):
        return jnp.where(x < 0, x + total, x)

    packed = me * rows + shift + lax.broadcasted_iota(jnp.int32, (rank, rows), 1)
    packed = jnp.where(packed >= total, packed - total, packed)
    inner = inner_ref[...].astype(jnp.float32)
    slots = [jnp.zeros_like(inner) for _ in range(3)]
    weights = [jnp.int32(0)] * 2
    flag = jnp.int32(0)
    for k in range(docs):
        mine = ((k & 1) ^ flip) == first_bit
        near = (k >> 1) == second_bit
        belongs = [mine & near, mine & jnp.logical_not(near), jnp.logical_not(mine)]
        inside = (packed >= starts[k]) & (packed < starts[k] + lengths[k])
        rows_of = jnp.where(inside, inner, 0.0)
        for i in range(3):
            slots[i] = slots[i] + jnp.where(belongs[i], 1.0, 0.0) * rows_of
        ahead, behind = firsts[k] - other * rows, other * rows - firsts[k]
        present = (wrapped(ahead) < rows) | (wrapped(behind) < lengths[k])
        for i in range(2):
            weights[i] = weights[i] + jnp.where(belongs[i] & present, 1, 0)
        flag = flag + jnp.where(belongs[0], inc_ref[0, k], 0)
    for i in range(3):
        spread[i * rank : (i + 1) * rank, :] = slots[i].astype(jnp.bfloat16)
    document = 2 * second_bit + (first_bit ^ flip)
    line = lax.broadcasted_iota(jnp.int32, flag_ref.shape, 0)
    facts = jnp.zeros(flag_ref.shape, jnp.float32)
    for i, fact in enumerate([flag, weights[0], weights[1], document]):
        facts = jnp.where(line == i, fact.astype(jnp.float32), facts)
    flag_ref[...] = facts
    left = spread[...]
    for j in range(chunks):
        copies[j].wait()
        product = jnp.dot(left, grad_buf[j], preferred_element_type=jnp.float32)
        columns = slice(j * width, (j + 1) * width)
        keep_ref[0, :, columns] = product[:rank]
        keep_ref[1, :, columns] = product[rank : 2 * rank]
        at = j * width % part
        send_refs[j * width // part][:, at : at + width] = product[2 * rank :]


def fold_kernel(half, keep_ref, recv_ref, fact_ref, send_ref, left_ref):
    width = send_ref.shape[1]
    columns = slice(half * width, (half + 1) * width)
    received = recv_ref[...]
    send_ref[...] = keep_ref[1, :, columns] + fact_ref[2:3, 0:1] * received
    left_ref[...] = keep_ref[0, :, columns] + fact_ref[1:2, 0:1] * received


def round_kernel(keep_ref, recv_ref, own_ref, mine_ref):
    own = keep_ref[...] + recv_ref[...]
    own_ref[...] = own
    mine_ref[...] = own.astype(jnp.bfloat16)


def swapped(pieces, bit):
    half = len(pieces) // 2
    low, high = pieces[:half], pieces[half:]
    first = [jnp.where(bit == 1, b, a) for a, b in zip(low, high)]
    second = [jnp.where(bit == 1, a, b) for a, b in zip(low, high)]
    return first, second


def relative(pieces, low):
    if len(pieces) == 1:
        return pieces
    first, second = swapped(pieces, (low >> (bits_of(len(pieces)) - 1)) & 1)
    return relative(first, low) + relative(second, low)


def gather(own_ref, mine_ref, other_ref):
    other = other_ref[...].astype(jnp.float32)
    seen = mine_ref[...].astype(jnp.float32) + other
    return own_ref[...] + other, jnp.sum(seen * seen, keepdims=True)


def gather_kernel(own_ref, mine_ref, other_ref, whole_ref, square_ref):
    whole, square = gather(own_ref, mine_ref, other_ref)
    whole_ref[...] = whole
    square_ref[...] = jnp.broadcast_to(square, square_ref.shape)


def clip_kernel(sending, n_dp, n_ctx, parts, *refs):
    whole_refs, square_refs = refs[: parts - 1], refs[parts - 1 : 2 * (parts - 1)]
    own_ref, mine_ref, other_ref, flag_ref, pieces_ref, *norm_refs = refs[2 * (parts - 1) :]
    slab = pieces_ref.shape[2]
    span = 2 * slab
    places = n_ctx // 2
    width = slab // places
    last, square = gather(own_ref, mine_ref, other_ref)
    wholes = [ref[...] for ref in whole_refs] + [last]
    for ref in square_refs:
        square = square + ref[0:1, 0:1]
    norm = jnp.sqrt(square)
    factor = flag_ref[0:1, 0:1] * clip_norm / jnp.maximum(norm, clip_norm)
    me = lax.axis_index("ctx")
    upper = me // places == 1
    low = lax.rem(me, places)
    dp = lax.axis_index("dp")
    core, chip = lax.rem(dp, 2), dp // 2
    halves = []
    for d in range(n_dp):
        whole = wholes[d * parts // n_dp]
        base = d % (n_dp // parts) * span
        halves.append(
            jnp.where(upper, whole[:, base + slab : base + span], whole[:, base : base + slab])
        )
    for x in range(n_dp // 2):
        piece = jnp.where(core == sending, halves[2 * x], halves[2 * x + 1])
        pieces = relative([piece[:, q * width : (q + 1) * width] for q in range(places)], low)
        pieces_ref[chip ^ x] = jnp.concatenate(pieces, axis=1) * factor
    for norm_ref in norm_refs:
        rows = lax.broadcasted_iota(jnp.int32, norm_ref.shape, 0).astype(jnp.float32)
        norm_ref[...] = jnp.where(rows == flag_ref[3:4, :], norm, 0.0)


def core_kernel(keep_ref, recv_ref, send_ref):
    send_ref[...] = keep_ref[1] + recv_ref[1]


def with_norms(block, norms, send_ref):
    width = block.shape[1]
    spare = send_ref.shape[1] - width
    send_ref[...] = jnp.concatenate([block, norms[:, :spare]], axis=1)


def chip_kernel(keep_ref, core_ref, recv_ref, norm_ref, send_ref, left_ref):
    total = keep_ref[0] + core_ref[0] + recv_ref[...]
    half = total.shape[1] // 2
    left_ref[...] = total[:, :half]
    with_norms(total[:, half:], norm_ref[...], send_ref)


def step_kernel(keep_ref, recv_ref, norm_ref, send_ref, left_ref, norms_ref):
    width = keep_ref.shape[1]
    half = width // 2
    received = recv_ref[...]
    total = keep_ref[...] + received[:, :width]
    norms = norm_ref[...] + received[:, width : width + 1]
    left_ref[...] = total[:, :half]
    norms_ref[...] = norms
    with_norms(total[:, half:], norms, send_ref)


def last_kernel(docs, keep_ref, recv_ref, norm_ref, out_ref, norms_ref):
    width = keep_ref.shape[1]
    received = recv_ref[...]
    out_ref[...] = keep_ref[...] + received[:, :width]
    norms = norm_ref[...] + received[:, width : width + 1]
    rows = lax.broadcasted_iota(jnp.int32, norms.shape, 0)
    lanes = lax.broadcasted_iota(jnp.int32, norms.shape, 1)
    norms_ref[...] = jnp.sum(jnp.where(rows == lanes, norms, 0.0), axis=0, keepdims=True)[:, :docs]


def exchange(block, n_dp, n_ctx, even_bit, odd_bit):
    route = [
        (d * n_ctx + c, d * n_ctx + (c ^ (1 << (odd_bit if d % 2 else even_bit))))
        for d in range(n_dp)
        for c in range(n_ctx)
    ]
    return lax.ppermute(block, ("dp", "ctx"), route)


def swap_dp(block, n_dp, bit):
    return lax.ppermute(block, "dp", [(d, d ^ (1 << bit)) for d in range(n_dp)])


def in_vmem(kernel, shapes, *operands, scalars=()):
    vmem = pl.BlockSpec(memory_space=pltpu.VMEM)
    smem = pl.BlockSpec(memory_space=pltpu.SMEM)
    return pl.pallas_call(
        kernel,
        out_shape=[pltpu.VMEM(shape, dtype) for shape, dtype in shapes],
        in_specs=[smem] * len(scalars) + [vmem] * len(operands),
        out_specs=[vmem] * len(shapes),
    )(*scalars, *[pltpu.with_memory_space_constraint(x, pltpu.VMEM) for x in operands])


def halving_plan(out_grad, adapter_inner, doc_lengths, slab_offset, included):
    n_dp, n_ctx = lax.axis_size("dp"), lax.axis_size("ctx")
    rows, features = out_grad.shape
    rank = adapter_inner.shape[1]
    docs = doc_lengths.shape[1]
    f32 = jnp.float32
    vmem = pl.BlockSpec(memory_space=pltpu.VMEM)
    hbm = pl.BlockSpec(memory_space=pl.ANY)
    parts = PARTS
    part = features // parts
    chunks = max(1, features // 1152)
    column = ((rank, 128), f32)
    single = ((rank, part), f32)

    *sends, keep, flag = pl.pallas_call(
        functools.partial(partials_kernel, n_ctx, docs, chunks),
        out_shape=[
            *[pltpu.VMEM(*single)] * parts,
            pltpu.VMEM((2, rank, features), f32),
            pltpu.VMEM((8, 128), f32),
        ],
        in_specs=[hbm] * 5,
        out_specs=[vmem] * (parts + 2),
        scratch_shapes=[
            pltpu.VMEM((chunks, rows, features // chunks), jnp.bfloat16),
            pltpu.VMEM((rank, rows), jnp.bfloat16),
            pltpu.VMEM((3 * rank, rows), jnp.bfloat16),
            pltpu.SMEM(doc_lengths.shape, jnp.int32),
            pltpu.SMEM((1, 1), jnp.int32),
            pltpu.SMEM(included.shape, jnp.int32),
            pltpu.SemaphoreType.DMA((4,)),
            pltpu.SemaphoreType.DMA((chunks,)),
        ],
        cost_estimate=pl.CostEstimate(
            flops=2 * 3 * rank * rows * features,
            bytes_accessed=2 * rows * features,
            transcendentals=0,
        ),
    )(doc_lengths, slab_offset[:, None], included, adapter_inner.T, out_grad)

    even, odd = halving_orders(n_ctx)
    rounds = list(zip(even, odd))
    wholes, squares = [], []
    firsts = [exchange(send, n_dp, n_ctx, *rounds[0]) for send in sends]
    for half in range(parts):
        send, left = in_vmem(
            functools.partial(fold_kernel, half), [single, single], keep, firsts[half], flag
        )
        received = exchange(send, n_dp, n_ctx, *rounds[1])
        own, mine = in_vmem(
            round_kernel, [single, ((rank, part), jnp.bfloat16)], left, received
        )
        other = exchange(mine, n_dp, n_ctx, *rounds[-1])
        if half < parts - 1:
            whole, square = in_vmem(gather_kernel, [single, ((8, 128), f32)], own, mine, other)
            wholes.append(whole)
            squares.append(square)
    slab = features // (2 * n_dp)
    pieces = ((n_dp // 2, rank, slab), f32)
    document = (*wholes, *squares, own, mine, other, flag)
    clip = functools.partial(clip_kernel, 1, n_dp, n_ctx, parts)
    (send,) = in_vmem(clip, [pieces], *document)
    clip = functools.partial(clip_kernel, 0, n_dp, n_ctx, parts)
    keep, norms = in_vmem(clip, [pieces, column], *document)
    core = swap_dp(send, n_dp, 0)
    (send,) = in_vmem(core_kernel, [((rank, slab), f32)], keep, core)
    received = swap_dp(send, n_dp, 1)

    def shapes(width):
        return [((rank, width // 128 * 128 + 128), f32), ((rank, width), f32)]

    width = slab // 2
    steps = list(reversed(range(bits_of(n_ctx // 2))))
    send, keep = in_vmem(chip_kernel, shapes(width), keep, core, received, norms)
    for bit in steps[:-1]:
        width //= 2
        received = exchange(send, n_dp, n_ctx, bit, bit)
        send, keep, norms = in_vmem(step_kernel, shapes(width) + [column], keep, received, norms)
    received = exchange(send, n_dp, n_ctx, steps[-1], steps[-1])
    result, norms = pl.pallas_call(
        functools.partial(last_kernel, docs),
        out_shape=[
            jax.ShapeDtypeStruct((rank, width), f32),
            jax.ShapeDtypeStruct((1, docs), f32),
        ],
        in_specs=[vmem] * 3,
        out_specs=[vmem, vmem],
    )(*[pltpu.with_memory_space_constraint(x, pltpu.VMEM) for x in (keep, received, norms)])
    return (result.T, norms)


def on_device(out_grad, adapter_inner, doc_lengths, slab_offset, included):
    n_dp, n_ctx = lax.axis_size("dp"), lax.axis_size("ctx")
    docs = doc_lengths.shape[1]
    rows = out_grad.shape[0]
    halving = (
        n_dp == 4
        and docs == 4
        and n_ctx == 2 * docs
        and docs <= adapter_inner.shape[1]
        and 2 * (rows - 2) + (docs - 2) * LONGEST < n_ctx * rows
        and out_grad.shape[1] % (1152 * PARTS) == 0
    )
    plan = halving_plan if halving else chain_plan
    return plan(out_grad, adapter_inner, doc_lengths, slab_offset, included)


def solution(mesh):
    placed = (P(("dp", "ctx"), None), P(("dp", "ctx"), None), P("dp", None), P("dp"), P("dp", None))
    return jax.shard_map(
        on_device,
        mesh=mesh,
        in_specs=placed,
        out_specs=(P(("dp", "ctx"), None), P("dp", None)),
        check_vma=False,
    )
```

```python
import functools

import jax
import jax.numpy as jnp
from jax import lax
from jax.experimental import pallas as pl
from jax.experimental.pallas import tpu as pltpu
from jax.sharding import PartitionSpec as P

SPAN = 3
PARTS = 2
LONGEST = 1536


clip_norm = 128.0


def from_behind(block, axis, distance):
    devices = range(lax.axis_size(axis))
    route = [((i - distance) % len(devices), i) for i in devices]
    return lax.ppermute(block, axis, route)


def document_ids(lengths, offset, positions, all_tokens):
    doc_ends = jnp.cumsum(lengths)
    starts = doc_ends - lengths
    longest = jnp.argmax(lengths)
    labels = jnp.arange(lengths.shape[0], dtype=jnp.int32)
    doc_shift = jnp.sum(jnp.where(labels == longest, starts, 0)) + offset
    packed = (positions + doc_shift) % all_tokens
    return jnp.sum((doc_ends[None, :] <= packed[:, None]).astype(jnp.int32), axis=1)


def pair_terms(
    left_ids, left_inner, left_grad, right_ids, right_inner, right_grad, keep_rows, member
):
    inner_gram = jnp.einsum(
        "ir,jr->ij", left_inner, right_inner, preferred_element_type=jnp.float32
    )
    grad_gram = jnp.einsum("id,jd->ij", left_grad, right_grad, preferred_element_type=jnp.float32)
    same_doc = (left_ids[:, None] == right_ids[None, :]) & keep_rows[:, None]
    weight = jnp.sum(jnp.where(same_doc, inner_gram * grad_gram, 0.0), axis=1)
    return jnp.dot(weight, member, precision=lax.Precision.HIGHEST)


def boundary_crossing_plan(
    ids_of, local_document_index, adapter_inner, out_grad, member, my_block, block_rows, all_tokens
):
    first_doc = local_document_index[0]
    last_doc = local_document_index[block_rows - 1]
    before_id = ids_of(jnp.reshape((my_block * block_rows - 1) % all_tokens, (1,)))[0]
    after_id = ids_of(jnp.reshape((my_block + 1) * block_rows % all_tokens, (1,)))[0]
    starts_before = before_id == first_doc
    continues = after_id == last_doc
    crossing = starts_before & (local_document_index == first_doc) | continues & (
        local_document_index == last_doc
    )
    norm_terms = pair_terms(
        local_document_index,
        adapter_inner,
        out_grad,
        local_document_index,
        adapter_inner,
        out_grad,
        jnp.logical_not(crossing),
        member,
    )
    in_first = (local_document_index == first_doc).astype(jnp.bfloat16)
    in_last = (local_document_index == last_doc).astype(jnp.bfloat16)
    first_part = jnp.einsum(
        "tr,td->rd", adapter_inner * in_first[:, None], out_grad, preferred_element_type=jnp.float32
    )
    last_part = jnp.einsum(
        "tr,td->rd", adapter_inner * in_last[:, None], out_grad, preferred_element_type=jnp.float32
    )
    finish = (starts_before & jnp.logical_not((first_doc == last_doc) & continues)).astype(
        jnp.float32
    )
    return (first_doc, last_doc, starts_before, norm_terms, first_part, last_part, finish)


def chain_plan(out_grad, adapter_inner, doc_lengths, slab_offset, included):
    block_rows = out_grad.shape[0]
    ctx_size = lax.axis_size("ctx")
    my_block = lax.axis_index("ctx")
    all_tokens = ctx_size * block_rows
    lengths = doc_lengths[0]
    doc_count = lengths.shape[0]
    row_index = jnp.arange(block_rows, dtype=jnp.int32)
    labels = jnp.arange(doc_count, dtype=jnp.int32)

    def ids_of(positions):
        return document_ids(lengths, slab_offset[0], positions, all_tokens)

    local_document_index = ids_of(my_block * block_rows + row_index)
    member = (local_document_index[:, None] == labels[None, :]).astype(jnp.float32)
    first_doc, last_doc, starts_before, norm_terms, first_part, last_part, finish = (
        boundary_crossing_plan(
            ids_of,
            local_document_index,
            adapter_inner,
            out_grad,
            member,
            my_block,
            block_rows,
            all_tokens,
        )
    )
    chain_flag = (starts_before & (first_doc == last_doc)).astype(jnp.float32)
    running = last_part
    received = jnp.zeros_like(last_part)
    for distance in range(SPAN):
        received = from_behind(running, "ctx", 1)
        running = last_part + chain_flag * received
    complete_document = received + first_part
    end_term = finish * jnp.sum(complete_document * complete_document)
    norm_terms = norm_terms + end_term * (labels == first_doc).astype(jnp.float32)
    squares = lax.psum(norm_terms, "ctx")
    document_grad_norm = jnp.sqrt(squares)
    clip_factor = (
        included[0].astype(jnp.float32) * clip_norm / jnp.maximum(document_grad_norm, clip_norm)
    )
    token_factor = jnp.dot(member, clip_factor, precision=lax.Precision.HIGHEST)
    scaled = (token_factor[:, None] * adapter_inner.astype(jnp.float32)).astype(jnp.bfloat16)
    adapter_second_gradient = lax.psum_scatter(
        jnp.einsum("td,tr->dr", out_grad, scaled, preferred_element_type=jnp.float32),
        ("dp", "ctx"),
        scatter_dimension=0,
        tiled=True,
    )
    return (adapter_second_gradient, document_grad_norm[None, :])


def bits_of(n):
    return n.bit_length() - 1


def halving_orders(n_ctx):
    even = list(range(bits_of(n_ctx)))
    odd = list(even)
    odd[0], odd[1] = odd[1], odd[0]
    return even, odd


def bit_in_use(block, place, n_ctx):
    odd = lax.rem(lax.axis_index("dp"), 2) == 1
    even_order, odd_order = halving_orders(n_ctx)
    return jnp.where(odd, (block >> odd_order[place]) & 1, (block >> even_order[place]) & 1)


def partials_kernel(
    n_ctx, docs, chunks, len_hbm, off_hbm, inc_hbm, inner_hbm, grad_hbm, *refs
):
    send_refs, (keep_ref, flag_ref, grad_buf, inner_ref, spread) = refs[:PARTS], refs[PARTS : PARTS + 5]
    len_ref, off_ref, inc_ref, small_sems, sems = refs[PARTS + 5 :]
    rank, rows = inner_ref.shape
    part = send_refs[0].shape[1]
    width = grad_hbm.shape[1] // chunks
    small = [
        pltpu.make_async_copy(len_hbm, len_ref, small_sems.at[0]),
        pltpu.make_async_copy(off_hbm, off_ref, small_sems.at[1]),
        pltpu.make_async_copy(inner_hbm, inner_ref, small_sems.at[2]),
        pltpu.make_async_copy(inc_hbm, inc_ref, small_sems.at[3]),
    ]
    copies = [
        pltpu.make_async_copy(
            grad_hbm.at[:, pl.ds(j * width, width)], grad_buf.at[j], sems.at[j]
        )
        for j in range(chunks)
    ]
    for copy in small + copies:
        copy.start()
    for copy in small:
        copy.wait()
    total = n_ctx * rows
    me = lax.axis_index("ctx")
    lengths = [len_ref[0, k] for k in range(docs)]
    starts = [jnp.int32(0)]
    for k in range(1, docs):
        starts.append(starts[-1] + lengths[k - 1])
    longest, best = starts[0], lengths[0]
    for k in range(1, docs):
        better = lengths[k] > best
        longest = jnp.where(better, starts[k], longest)
        best = jnp.where(better, lengths[k], best)
    shift = longest + off_ref[0, 0]
    firsts = []
    for k in range(docs):
        first = starts[k] - shift
        firsts.append(jnp.where(first < 0, first + total, first))
    flip = jnp.int32(0)
    for k in range(docs):
        block = lax.div(firsts[k], jnp.int32(rows))
        offset = firsts[k] - block * rows
        inside = (offset >= 1) & (offset + lengths[k] <= rows - 1)
        flip = flip + jnp.where(inside, ((k + 1) & 1) ^ bit_in_use(block, 0, n_ctx), 0)
    first_bit, second_bit = bit_in_use(me, 0, n_ctx), bit_in_use(me, 1, n_ctx)
    even_order, odd_order = halving_orders(n_ctx)
    odd = lax.rem(lax.axis_index("dp"), 2) == 1
    other = me ^ jnp.where(odd, 1 << odd_order[0], 1 << even_order[0])

    def wrapped(x):
        return jnp.where(x < 0, x + total, x)

    packed = me * rows + shift + lax.broadcasted_iota(jnp.int32, (rank, rows), 1)
    packed = jnp.where(packed >= total, packed - total, packed)
    inner = inner_ref[...].astype(jnp.float32)
    slots = [jnp.zeros_like(inner) for _ in range(3)]
    weights = [jnp.int32(0)] * 2
    flag = jnp.int32(0)
    for k in range(docs):
        mine = ((k & 1) ^ flip) == first_bit
        near = (k >> 1) == second_bit
        belongs = [mine & near, mine & jnp.logical_not(near), jnp.logical_not(mine)]
        inside = (packed >= starts[k]) & (packed < starts[k] + lengths[k])
        rows_of = jnp.where(inside, inner, 0.0)
        for i in range(3):
            slots[i] = slots[i] + jnp.where(belongs[i], 1.0, 0.0) * rows_of
        ahead, behind = firsts[k] - other * rows, other * rows - firsts[k]
        present = (wrapped(ahead) < rows) | (wrapped(behind) < lengths[k])
        for i in range(2):
            weights[i] = weights[i] + jnp.where(belongs[i] & present, 1, 0)
        flag = flag + jnp.where(belongs[0], inc_ref[0, k], 0)
    for i in range(3):
        spread[i * rank : (i + 1) * rank, :] = slots[i].astype(jnp.bfloat16)
    document = 2 * second_bit + (first_bit ^ flip)
    line = lax.broadcasted_iota(jnp.int32, flag_ref.shape, 0)
    facts = jnp.zeros(flag_ref.shape, jnp.float32)
    for i, fact in enumerate([flag, weights[0], weights[1], document]):
        facts = jnp.where(line == i, fact.astype(jnp.float32), facts)
    flag_ref[...] = facts
    left = spread[...]
    for j in range(chunks):
        copies[j].wait()
        product = jnp.dot(left, grad_buf[j], preferred_element_type=jnp.float32)
        columns = slice(j * width, (j + 1) * width)
        keep_ref[0, :, columns] = product[:rank]
        keep_ref[1, :, columns] = product[rank : 2 * rank]
        at = j * width % part
        send_refs[j * width // part][:, at : at + width] = product[2 * rank :]


def fold_kernel(half, place, keep_ref, recv_ref, fact_ref, out_ref):
    width = out_ref.shape[1]
    columns = slice(half * width, (half + 1) * width)
    weight = fact_ref[place + 1 : place + 2, 0:1]
    out_ref[...] = keep_ref[place, :, columns] + weight * recv_ref[...]


def round_kernel(keep_ref, recv_ref, out_ref):
    out_ref[...] = (keep_ref[...] + recv_ref[...]).astype(out_ref.dtype)


def swapped(pieces, bit):
    half = len(pieces) // 2
    low, high = pieces[:half], pieces[half:]
    first = [jnp.where(bit == 1, b, a) for a, b in zip(low, high)]
    second = [jnp.where(bit == 1, a, b) for a, b in zip(low, high)]
    return first, second


def relative(pieces, low):
    if len(pieces) == 1:
        return pieces
    first, second = swapped(pieces, (low >> (bits_of(len(pieces)) - 1)) & 1)
    return relative(first, low) + relative(second, low)


def gather(own_ref, mine_ref, other_ref):
    other = other_ref[...].astype(jnp.float32)
    seen = mine_ref[...].astype(jnp.float32) + other
    return own_ref[...] + other, jnp.sum(seen * seen, keepdims=True)


def gather_kernel(own_ref, mine_ref, other_ref, whole_ref, square_ref):
    whole, square = gather(own_ref, mine_ref, other_ref)
    whole_ref[...] = whole
    square_ref[...] = jnp.broadcast_to(square, square_ref.shape)


def clip_kernel(sending, n_dp, n_ctx, parts, *refs):
    whole_refs, square_refs = refs[: parts - 1], refs[parts - 1 : 2 * (parts - 1)]
    own_ref, mine_ref, other_ref, flag_ref, pieces_ref, *norm_refs = refs[2 * (parts - 1) :]
    slab = pieces_ref.shape[2]
    span = 2 * slab
    places = n_ctx // 2
    width = slab // places
    last, square = gather(own_ref, mine_ref, other_ref)
    wholes = [ref[...] for ref in whole_refs] + [last]
    for ref in square_refs:
        square = square + ref[0:1, 0:1]
    norm = jnp.sqrt(square)
    factor = flag_ref[0:1, 0:1] * clip_norm / jnp.maximum(norm, clip_norm)
    me = lax.axis_index("ctx")
    upper = me // places == 1
    low = lax.rem(me, places)
    dp = lax.axis_index("dp")
    core, chip = lax.rem(dp, 2), dp // 2
    halves = []
    for d in range(n_dp):
        whole = wholes[d * parts // n_dp]
        base = d % (n_dp // parts) * span
        halves.append(
            jnp.where(upper, whole[:, base + slab : base + span], whole[:, base : base + slab])
        )
    for x in range(n_dp // 2):
        piece = jnp.where(core == sending, halves[2 * x], halves[2 * x + 1])
        pieces = relative([piece[:, q * width : (q + 1) * width] for q in range(places)], low ^ (places - 1))
        pieces_ref[chip ^ x] = jnp.concatenate(pieces, axis=1) * factor
    for norm_ref in norm_refs:
        rows = lax.broadcasted_iota(jnp.int32, norm_ref.shape, 0).astype(jnp.float32)
        norm_ref[...] = jnp.where(rows == flag_ref[3:4, :], norm, 0.0)


def core_kernel(keep_ref, recv_ref, send_ref):
    send_ref[...] = keep_ref[1] + recv_ref[1]


def with_norms(total, norms, send_ref):
    lanes = lax.broadcasted_iota(jnp.int32, send_ref.shape, 1)
    send_ref[...] = jnp.where(
        lanes < total.shape[1] // 2, total[:, : send_ref.shape[1]], norms[:, 0:1]
    )


def chip_total(keep_ref, core_ref, recv_ref):
    return keep_ref[0] + core_ref[0] + recv_ref[...]


def chip_send_kernel(keep_ref, core_ref, recv_ref, norm_ref, send_ref):
    with_norms(chip_total(keep_ref, core_ref, recv_ref), norm_ref[...], send_ref)


def chip_left_kernel(keep_ref, core_ref, recv_ref, left_ref):
    left_ref[...] = chip_total(keep_ref, core_ref, recv_ref)[:, left_ref.shape[1] :]


def step_total(keep_ref, recv_ref, norm_ref):
    width = keep_ref.shape[1]
    received = recv_ref[...]
    return keep_ref[...] + received[:, :width], norm_ref[...] + received[:, width : width + 1]


def step_send_kernel(keep_ref, recv_ref, norm_ref, send_ref):
    with_norms(*step_total(keep_ref, recv_ref, norm_ref), send_ref)


def step_left_kernel(keep_ref, recv_ref, norm_ref, left_ref, norms_ref):
    total, norms = step_total(keep_ref, recv_ref, norm_ref)
    left_ref[...] = total[:, left_ref.shape[1] :]
    norms_ref[...] = norms


def last_kernel(docs, keep_ref, recv_ref, norm_ref, out_ref, norms_ref):
    width = keep_ref.shape[1]
    received = recv_ref[...]
    out_ref[...] = keep_ref[...] + received[:, :width]
    norms = norm_ref[...] + received[:, width : width + 1]
    rows = lax.broadcasted_iota(jnp.int32, norms.shape, 0)
    lanes = lax.broadcasted_iota(jnp.int32, norms.shape, 1)
    norms_ref[...] = jnp.sum(jnp.where(rows == lanes, norms, 0.0), axis=0, keepdims=True)[:, :docs]


def exchange(block, n_dp, n_ctx, even_bit, odd_bit):
    route = [
        (d * n_ctx + c, d * n_ctx + (c ^ (1 << (odd_bit if d % 2 else even_bit))))
        for d in range(n_dp)
        for c in range(n_ctx)
    ]
    return lax.ppermute(block, ("dp", "ctx"), route)


def swap_dp(block, n_dp, bit):
    return lax.ppermute(block, "dp", [(d, d ^ (1 << bit)) for d in range(n_dp)])


def in_vmem(kernel, shapes, *operands, scalars=()):
    vmem = pl.BlockSpec(memory_space=pltpu.VMEM)
    smem = pl.BlockSpec(memory_space=pltpu.SMEM)
    return pl.pallas_call(
        kernel,
        out_shape=[pltpu.VMEM(shape, dtype) for shape, dtype in shapes],
        in_specs=[smem] * len(scalars) + [vmem] * len(operands),
        out_specs=[vmem] * len(shapes),
    )(*scalars, *[pltpu.with_memory_space_constraint(x, pltpu.VMEM) for x in operands])


def halving_plan(out_grad, adapter_inner, doc_lengths, slab_offset, included):
    n_dp, n_ctx = lax.axis_size("dp"), lax.axis_size("ctx")
    rows, features = out_grad.shape
    rank = adapter_inner.shape[1]
    docs = doc_lengths.shape[1]
    f32 = jnp.float32
    vmem = pl.BlockSpec(memory_space=pltpu.VMEM)
    hbm = pl.BlockSpec(memory_space=pl.ANY)
    parts = PARTS
    part = features // parts
    chunks = max(1, features // 1152)
    column = ((rank, 128), f32)
    single = ((rank, part), f32)

    *sends, keep, flag = pl.pallas_call(
        functools.partial(partials_kernel, n_ctx, docs, chunks),
        out_shape=[
            *[pltpu.VMEM(*single)] * parts,
            pltpu.VMEM((2, rank, features), f32),
            pltpu.VMEM((8, 128), f32),
        ],
        in_specs=[hbm] * 5,
        out_specs=[vmem] * (parts + 2),
        scratch_shapes=[
            pltpu.VMEM((chunks, rows, features // chunks), jnp.bfloat16),
            pltpu.VMEM((rank, rows), jnp.bfloat16),
            pltpu.VMEM((3 * rank, rows), jnp.bfloat16),
            pltpu.SMEM(doc_lengths.shape, jnp.int32),
            pltpu.SMEM((1, 1), jnp.int32),
            pltpu.SMEM(included.shape, jnp.int32),
            pltpu.SemaphoreType.DMA((4,)),
            pltpu.SemaphoreType.DMA((chunks,)),
        ],
        cost_estimate=pl.CostEstimate(
            flops=2 * 3 * rank * rows * features,
            bytes_accessed=2 * rows * features,
            transcendentals=0,
        ),
    )(doc_lengths, slab_offset[:, None], included, adapter_inner.T, out_grad)

    even, odd = halving_orders(n_ctx)
    rounds = list(zip(even, odd))
    wholes, squares = [], []
    firsts = [exchange(send, n_dp, n_ctx, *rounds[0]) for send in sends]
    for half in range(parts):
        pair = (keep, firsts[half], flag)
        (send,) = in_vmem(functools.partial(fold_kernel, half, 1), [single], *pair)
        received = exchange(send, n_dp, n_ctx, *rounds[1])
        (left,) = in_vmem(functools.partial(fold_kernel, half, 0), [single], *pair)
        (mine,) = in_vmem(round_kernel, [((rank, part), jnp.bfloat16)], left, received)
        (own,) = in_vmem(round_kernel, [single], left, received)
        other = exchange(mine, n_dp, n_ctx, *rounds[-1])
        if half < parts - 1:
            whole, square = in_vmem(gather_kernel, [single, ((8, 128), f32)], own, mine, other)
            wholes.append(whole)
            squares.append(square)
    slab = features // (2 * n_dp)
    pieces = ((n_dp // 2, rank, slab), f32)
    document = (*wholes, *squares, own, mine, other, flag)
    clip = functools.partial(clip_kernel, 1, n_dp, n_ctx, parts)
    (send,) = in_vmem(clip, [pieces], *document)
    clip = functools.partial(clip_kernel, 0, n_dp, n_ctx, parts)
    keep, norms = in_vmem(clip, [pieces, column], *document)
    core = swap_dp(send, n_dp, 0)
    (send,) = in_vmem(core_kernel, [((rank, slab), f32)], keep, core)
    received = swap_dp(send, n_dp, 1)

    def shapes(width):
        return [((rank, width // 128 * 128 + 128), f32), ((rank, width), f32)]

    width = slab // 2
    steps = list(reversed(range(bits_of(n_ctx // 2))))
    wide, narrow = shapes(width)
    (send,) = in_vmem(chip_send_kernel, [wide], keep, core, received, norms)
    (keep,) = in_vmem(chip_left_kernel, [narrow], keep, core, received)
    for bit in steps[:-1]:
        width //= 2
        received = exchange(send, n_dp, n_ctx, bit, bit)
        wide, narrow = shapes(width)
        (send,) = in_vmem(step_send_kernel, [wide], keep, received, norms)
        keep, norms = in_vmem(step_left_kernel, [narrow, column], keep, received, norms)
    received = exchange(send, n_dp, n_ctx, steps[-1], steps[-1])
    result, norms = pl.pallas_call(
        functools.partial(last_kernel, docs),
        out_shape=[
            jax.ShapeDtypeStruct((rank, width), f32),
            jax.ShapeDtypeStruct((1, docs), f32),
        ],
        in_specs=[vmem] * 3,
        out_specs=[vmem, vmem],
    )(*[pltpu.with_memory_space_constraint(x, pltpu.VMEM) for x in (keep, received, norms)])
    return (result.T, norms)


def on_device(out_grad, adapter_inner, doc_lengths, slab_offset, included):
    n_dp, n_ctx = lax.axis_size("dp"), lax.axis_size("ctx")
    docs = doc_lengths.shape[1]
    rows = out_grad.shape[0]
    halving = (
        n_dp == 4
        and docs == 4
        and n_ctx == 2 * docs
        and docs <= adapter_inner.shape[1]
        and 2 * (rows - 2) + (docs - 2) * LONGEST < n_ctx * rows
        and out_grad.shape[1] % (1152 * PARTS) == 0
    )
    plan = halving_plan if halving else chain_plan
    return plan(out_grad, adapter_inner, doc_lengths, slab_offset, included)


def solution(mesh):
    placed = (P(("dp", "ctx"), None), P(("dp", "ctx"), None), P("dp", None), P("dp"), P("dp", None))
    return jax.shard_map(
        on_device,
        mesh=mesh,
        in_specs=placed,
        out_specs=(P(("dp", "ctx"), None), P("dp", None)),
        check_vma=False,
    )
```

```python
import functools

import jax
import jax.numpy as jnp
from jax import lax
from jax.experimental import pallas as pl
from jax.experimental.pallas import tpu as pltpu
from jax.sharding import PartitionSpec as P

SPAN = 3
PARTS = 2
LONGEST = 1536


clip_norm = 128.0


def from_behind(block, axis, distance):
    devices = range(lax.axis_size(axis))
    route = [((i - distance) % len(devices), i) for i in devices]
    return lax.ppermute(block, axis, route)


def document_ids(lengths, offset, positions, all_tokens):
    doc_ends = jnp.cumsum(lengths)
    starts = doc_ends - lengths
    longest = jnp.argmax(lengths)
    labels = jnp.arange(lengths.shape[0], dtype=jnp.int32)
    doc_shift = jnp.sum(jnp.where(labels == longest, starts, 0)) + offset
    packed = (positions + doc_shift) % all_tokens
    return jnp.sum((doc_ends[None, :] <= packed[:, None]).astype(jnp.int32), axis=1)


def pair_terms(
    left_ids, left_inner, left_grad, right_ids, right_inner, right_grad, keep_rows, member
):
    inner_gram = jnp.einsum(
        "ir,jr->ij", left_inner, right_inner, preferred_element_type=jnp.float32
    )
    grad_gram = jnp.einsum("id,jd->ij", left_grad, right_grad, preferred_element_type=jnp.float32)
    same_doc = (left_ids[:, None] == right_ids[None, :]) & keep_rows[:, None]
    weight = jnp.sum(jnp.where(same_doc, inner_gram * grad_gram, 0.0), axis=1)
    return jnp.dot(weight, member, precision=lax.Precision.HIGHEST)


def boundary_crossing_plan(
    ids_of, local_document_index, adapter_inner, out_grad, member, my_block, block_rows, all_tokens
):
    first_doc = local_document_index[0]
    last_doc = local_document_index[block_rows - 1]
    before_id = ids_of(jnp.reshape((my_block * block_rows - 1) % all_tokens, (1,)))[0]
    after_id = ids_of(jnp.reshape((my_block + 1) * block_rows % all_tokens, (1,)))[0]
    starts_before = before_id == first_doc
    continues = after_id == last_doc
    crossing = starts_before & (local_document_index == first_doc) | continues & (
        local_document_index == last_doc
    )
    norm_terms = pair_terms(
        local_document_index,
        adapter_inner,
        out_grad,
        local_document_index,
        adapter_inner,
        out_grad,
        jnp.logical_not(crossing),
        member,
    )
    in_first = (local_document_index == first_doc).astype(jnp.bfloat16)
    in_last = (local_document_index == last_doc).astype(jnp.bfloat16)
    first_part = jnp.einsum(
        "tr,td->rd", adapter_inner * in_first[:, None], out_grad, preferred_element_type=jnp.float32
    )
    last_part = jnp.einsum(
        "tr,td->rd", adapter_inner * in_last[:, None], out_grad, preferred_element_type=jnp.float32
    )
    finish = (starts_before & jnp.logical_not((first_doc == last_doc) & continues)).astype(
        jnp.float32
    )
    return (first_doc, last_doc, starts_before, norm_terms, first_part, last_part, finish)


def chain_plan(out_grad, adapter_inner, doc_lengths, slab_offset, included):
    block_rows = out_grad.shape[0]
    ctx_size = lax.axis_size("ctx")
    my_block = lax.axis_index("ctx")
    all_tokens = ctx_size * block_rows
    lengths = doc_lengths[0]
    doc_count = lengths.shape[0]
    row_index = jnp.arange(block_rows, dtype=jnp.int32)
    labels = jnp.arange(doc_count, dtype=jnp.int32)

    def ids_of(positions):
        return document_ids(lengths, slab_offset[0], positions, all_tokens)

    local_document_index = ids_of(my_block * block_rows + row_index)
    member = (local_document_index[:, None] == labels[None, :]).astype(jnp.float32)
    first_doc, last_doc, starts_before, norm_terms, first_part, last_part, finish = (
        boundary_crossing_plan(
            ids_of,
            local_document_index,
            adapter_inner,
            out_grad,
            member,
            my_block,
            block_rows,
            all_tokens,
        )
    )
    chain_flag = (starts_before & (first_doc == last_doc)).astype(jnp.float32)
    running = last_part
    received = jnp.zeros_like(last_part)
    for distance in range(SPAN):
        received = from_behind(running, "ctx", 1)
        running = last_part + chain_flag * received
    complete_document = received + first_part
    end_term = finish * jnp.sum(complete_document * complete_document)
    norm_terms = norm_terms + end_term * (labels == first_doc).astype(jnp.float32)
    squares = lax.psum(norm_terms, "ctx")
    document_grad_norm = jnp.sqrt(squares)
    clip_factor = (
        included[0].astype(jnp.float32) * clip_norm / jnp.maximum(document_grad_norm, clip_norm)
    )
    token_factor = jnp.dot(member, clip_factor, precision=lax.Precision.HIGHEST)
    scaled = (token_factor[:, None] * adapter_inner.astype(jnp.float32)).astype(jnp.bfloat16)
    adapter_second_gradient = lax.psum_scatter(
        jnp.einsum("td,tr->dr", out_grad, scaled, preferred_element_type=jnp.float32),
        ("dp", "ctx"),
        scatter_dimension=0,
        tiled=True,
    )
    return (adapter_second_gradient, document_grad_norm[None, :])


def bits_of(n):
    return n.bit_length() - 1


def halving_orders(n_ctx):
    even = list(range(bits_of(n_ctx)))
    odd = list(even)
    odd[0], odd[1] = odd[1], odd[0]
    return even, odd


def bit_in_use(block, place, n_ctx):
    odd = lax.rem(lax.axis_index("dp"), 2) == 1
    even_order, odd_order = halving_orders(n_ctx)
    return jnp.where(odd, (block >> odd_order[place]) & 1, (block >> even_order[place]) & 1)


def partials_kernel(
    n_ctx, docs, chunks, len_hbm, off_hbm, inc_hbm, inner_hbm, grad_hbm, *refs
):
    send_refs, (keep_ref, flag_ref, grad_buf, inner_ref, spread) = refs[:PARTS], refs[PARTS : PARTS + 5]
    len_ref, off_ref, inc_ref, small_sems, sems = refs[PARTS + 5 :]
    rank, rows = inner_ref.shape
    part = send_refs[0].shape[1]
    width = grad_hbm.shape[1] // chunks
    small = [
        pltpu.make_async_copy(len_hbm, len_ref, small_sems.at[0]),
        pltpu.make_async_copy(off_hbm, off_ref, small_sems.at[1]),
        pltpu.make_async_copy(inner_hbm, inner_ref, small_sems.at[2]),
        pltpu.make_async_copy(inc_hbm, inc_ref, small_sems.at[3]),
    ]
    copies = [
        pltpu.make_async_copy(
            grad_hbm.at[:, pl.ds(j * width, width)], grad_buf.at[j], sems.at[j]
        )
        for j in range(chunks)
    ]
    for copy in copies[:1] + small + copies[1:]:
        copy.start()
    for copy in small:
        copy.wait()
    total = n_ctx * rows
    me = lax.axis_index("ctx")
    lengths = [len_ref[0, k] for k in range(docs)]
    starts = [jnp.int32(0)]
    for k in range(1, docs):
        starts.append(starts[-1] + lengths[k - 1])
    longest, best = starts[0], lengths[0]
    for k in range(1, docs):
        better = lengths[k] > best
        longest = jnp.where(better, starts[k], longest)
        best = jnp.where(better, lengths[k], best)
    shift = longest + off_ref[0, 0]
    firsts = []
    for k in range(docs):
        first = starts[k] - shift
        firsts.append(jnp.where(first < 0, first + total, first))
    flip = jnp.int32(0)
    for k in range(docs):
        block = lax.div(firsts[k], jnp.int32(rows))
        offset = firsts[k] - block * rows
        inside = (offset >= 1) & (offset + lengths[k] <= rows - 1)
        flip = flip + jnp.where(inside, ((k + 1) & 1) ^ bit_in_use(block, 0, n_ctx), 0)
    first_bit, second_bit = bit_in_use(me, 0, n_ctx), bit_in_use(me, 1, n_ctx)
    even_order, odd_order = halving_orders(n_ctx)
    odd = lax.rem(lax.axis_index("dp"), 2) == 1
    other = me ^ jnp.where(odd, 1 << odd_order[0], 1 << even_order[0])

    def wrapped(x):
        return jnp.where(x < 0, x + total, x)

    packed = me * rows + shift + lax.broadcasted_iota(jnp.int32, (rank, rows), 1)
    packed = jnp.where(packed >= total, packed - total, packed)
    inner = inner_ref[...].astype(jnp.float32)
    slots = [jnp.zeros_like(inner) for _ in range(3)]
    weights = [jnp.int32(0)] * 2
    flag = jnp.int32(0)
    for k in range(docs):
        mine = ((k & 1) ^ flip) == first_bit
        near = (k >> 1) == second_bit
        belongs = [mine & near, mine & jnp.logical_not(near), jnp.logical_not(mine)]
        inside = (packed >= starts[k]) & (packed < starts[k] + lengths[k])
        rows_of = jnp.where(inside, inner, 0.0)
        for i in range(3):
            slots[i] = slots[i] + jnp.where(belongs[i], 1.0, 0.0) * rows_of
        ahead, behind = firsts[k] - other * rows, other * rows - firsts[k]
        present = (wrapped(ahead) < rows) | (wrapped(behind) < lengths[k])
        for i in range(2):
            weights[i] = weights[i] + jnp.where(belongs[i] & present, 1, 0)
        flag = flag + jnp.where(belongs[0], inc_ref[0, k], 0)
    for i in range(3):
        spread[i * rank : (i + 1) * rank, :] = slots[i].astype(jnp.bfloat16)
    document = 2 * second_bit + (first_bit ^ flip)
    line = lax.broadcasted_iota(jnp.int32, flag_ref.shape, 0)
    facts = jnp.zeros(flag_ref.shape, jnp.float32)
    for i, fact in enumerate([flag, weights[0], weights[1], document]):
        facts = jnp.where(line == i, fact.astype(jnp.float32), facts)
    flag_ref[...] = facts
    left = spread[...]
    for j in range(chunks):
        copies[j].wait()
        product = jnp.dot(left, grad_buf[j], preferred_element_type=jnp.float32)
        columns = slice(j * width, (j + 1) * width)
        keep_ref[0, :, columns] = product[:rank]
        keep_ref[1, :, columns] = product[rank : 2 * rank]
        at = j * width % part
        send_refs[j * width // part][:, at : at + width] = product[2 * rank :]


def fold_kernel(half, keep_ref, recv_ref, fact_ref, send_ref, left_ref):
    width = send_ref.shape[1]
    columns = slice(half * width, (half + 1) * width)
    received = recv_ref[...]
    send_ref[...] = keep_ref[1, :, columns] + fact_ref[2:3, 0:1] * received
    left_ref[...] = keep_ref[0, :, columns] + fact_ref[1:2, 0:1] * received


def round_kernel(keep_ref, recv_ref, own_ref, mine_ref):
    own = keep_ref[...] + recv_ref[...]
    own_ref[...] = own
    mine_ref[...] = own.astype(jnp.bfloat16)


def swapped(pieces, bit):
    half = len(pieces) // 2
    low, high = pieces[:half], pieces[half:]
    first = [jnp.where(bit == 1, b, a) for a, b in zip(low, high)]
    second = [jnp.where(bit == 1, a, b) for a, b in zip(low, high)]
    return first, second


def relative(pieces, low):
    if len(pieces) == 1:
        return pieces
    first, second = swapped(pieces, (low >> (bits_of(len(pieces)) - 1)) & 1)
    return relative(first, low) + relative(second, low)


def gather(own_ref, mine_ref, other_ref):
    other = other_ref[...].astype(jnp.float32)
    seen = mine_ref[...].astype(jnp.float32) + other
    return own_ref[...] + other, jnp.sum(seen * seen, keepdims=True)


def gather_kernel(own_ref, mine_ref, other_ref, whole_ref, square_ref):
    whole, square = gather(own_ref, mine_ref, other_ref)
    whole_ref[...] = whole
    square_ref[...] = jnp.broadcast_to(square, square_ref.shape)


def clip_kernel(sending, n_dp, n_ctx, parts, *refs):
    whole_refs, square_refs = refs[: parts - 1], refs[parts - 1 : 2 * (parts - 1)]
    own_ref, mine_ref, other_ref, flag_ref, pieces_ref, *norm_refs = refs[2 * (parts - 1) :]
    slab = pieces_ref.shape[2]
    span = 2 * slab
    places = n_ctx // 2
    width = slab // places
    last, square = gather(own_ref, mine_ref, other_ref)
    wholes = [ref[...] for ref in whole_refs] + [last]
    for ref in square_refs:
        square = square + ref[0:1, 0:1]
    norm = jnp.sqrt(square)
    factor = flag_ref[0:1, 0:1] * clip_norm / jnp.maximum(norm, clip_norm)
    me = lax.axis_index("ctx")
    upper = me // places == 1
    low = lax.rem(me, places)
    dp = lax.axis_index("dp")
    core, chip = lax.rem(dp, 2), dp // 2
    halves = []
    for d in range(n_dp):
        whole = wholes[d * parts // n_dp]
        base = d % (n_dp // parts) * span
        halves.append(
            jnp.where(upper, whole[:, base + slab : base + span], whole[:, base : base + slab])
        )
    for x in range(n_dp // 2):
        piece = jnp.where(core == sending, halves[2 * x], halves[2 * x + 1])
        pieces = relative([piece[:, q * width : (q + 1) * width] for q in range(places)], low)
        pieces_ref[chip ^ x] = jnp.concatenate(pieces, axis=1) * factor
    for norm_ref in norm_refs:
        rows = lax.broadcasted_iota(jnp.int32, norm_ref.shape, 0).astype(jnp.float32)
        norm_ref[...] = jnp.where(rows == flag_ref[3:4, :], norm, 0.0)


def core_kernel(keep_ref, recv_ref, send_ref):
    send_ref[...] = keep_ref[1] + recv_ref[1]


def with_norms(block, norms, send_ref):
    width = block.shape[1]
    spare = send_ref.shape[1] - width
    send_ref[...] = jnp.concatenate([block, norms[:, :spare]], axis=1)


def chip_kernel(keep_ref, core_ref, recv_ref, norm_ref, send_ref, left_ref):
    total = keep_ref[0] + core_ref[0] + recv_ref[...]
    half = total.shape[1] // 2
    left_ref[...] = total[:, :half]
    with_norms(total[:, half:], norm_ref[...], send_ref)


def step_kernel(keep_ref, recv_ref, norm_ref, send_ref, left_ref, norms_ref):
    width = keep_ref.shape[1]
    half = width // 2
    received = recv_ref[...]
    total = keep_ref[...] + received[:, :width]
    norms = norm_ref[...] + received[:, width : width + 1]
    left_ref[...] = total[:, :half]
    norms_ref[...] = norms
    with_norms(total[:, half:], norms, send_ref)


def last_kernel(docs, keep_ref, recv_ref, norm_ref, out_ref, norms_ref):
    width = keep_ref.shape[1]
    received = recv_ref[...]
    out_ref[...] = keep_ref[...] + received[:, :width]
    norms = norm_ref[...] + received[:, width : width + 1]
    rows = lax.broadcasted_iota(jnp.int32, norms.shape, 0)
    lanes = lax.broadcasted_iota(jnp.int32, norms.shape, 1)
    norms_ref[...] = jnp.sum(jnp.where(rows == lanes, norms, 0.0), axis=0, keepdims=True)[:, :docs]


def exchange(block, n_dp, n_ctx, even_bit, odd_bit):
    route = [
        (d * n_ctx + c, d * n_ctx + (c ^ (1 << (odd_bit if d % 2 else even_bit))))
        for d in range(n_dp)
        for c in range(n_ctx)
    ]
    return lax.ppermute(block, ("dp", "ctx"), route)


def swap_dp(block, n_dp, bit):
    return lax.ppermute(block, "dp", [(d, d ^ (1 << bit)) for d in range(n_dp)])


def in_vmem(kernel, shapes, *operands, scalars=()):
    vmem = pl.BlockSpec(memory_space=pltpu.VMEM)
    smem = pl.BlockSpec(memory_space=pltpu.SMEM)
    return pl.pallas_call(
        kernel,
        out_shape=[pltpu.VMEM(shape, dtype) for shape, dtype in shapes],
        in_specs=[smem] * len(scalars) + [vmem] * len(operands),
        out_specs=[vmem] * len(shapes),
    )(*scalars, *[pltpu.with_memory_space_constraint(x, pltpu.VMEM) for x in operands])


def halving_plan(out_grad, adapter_inner, doc_lengths, slab_offset, included):
    n_dp, n_ctx = lax.axis_size("dp"), lax.axis_size("ctx")
    rows, features = out_grad.shape
    rank = adapter_inner.shape[1]
    docs = doc_lengths.shape[1]
    f32 = jnp.float32
    vmem = pl.BlockSpec(memory_space=pltpu.VMEM)
    hbm = pl.BlockSpec(memory_space=pl.ANY)
    parts = PARTS
    part = features // parts
    chunks = max(1, features // 1152)
    column = ((rank, 128), f32)
    single = ((rank, part), f32)

    *sends, keep, flag = pl.pallas_call(
        functools.partial(partials_kernel, n_ctx, docs, chunks),
        out_shape=[
            *[pltpu.VMEM(*single)] * parts,
            pltpu.VMEM((2, rank, features), f32),
            pltpu.VMEM((8, 128), f32),
        ],
        in_specs=[hbm] * 5,
        out_specs=[vmem] * (parts + 2),
        scratch_shapes=[
            pltpu.VMEM((chunks, rows, features // chunks), jnp.bfloat16),
            pltpu.VMEM((rank, rows), jnp.bfloat16),
            pltpu.VMEM((3 * rank, rows), jnp.bfloat16),
            pltpu.SMEM(doc_lengths.shape, jnp.int32),
            pltpu.SMEM((1, 1), jnp.int32),
            pltpu.SMEM(included.shape, jnp.int32),
            pltpu.SemaphoreType.DMA((4,)),
            pltpu.SemaphoreType.DMA((chunks,)),
        ],
        cost_estimate=pl.CostEstimate(
            flops=2 * 3 * rank * rows * features,
            bytes_accessed=2 * rows * features,
            transcendentals=0,
        ),
    )(doc_lengths, slab_offset[:, None], included, adapter_inner.T, out_grad)

    even, odd = halving_orders(n_ctx)
    rounds = list(zip(even, odd))
    wholes, squares = [], []
    firsts = [exchange(send, n_dp, n_ctx, *rounds[0]) for send in sends]
    for half in range(parts):
        send, left = in_vmem(
            functools.partial(fold_kernel, half), [single, single], keep, firsts[half], flag
        )
        received = exchange(send, n_dp, n_ctx, *rounds[1])
        own, mine = in_vmem(
            round_kernel, [single, ((rank, part), jnp.bfloat16)], left, received
        )
        other = exchange(mine, n_dp, n_ctx, *rounds[-1])
        if half < parts - 1:
            whole, square = in_vmem(gather_kernel, [single, ((8, 128), f32)], own, mine, other)
            wholes.append(whole)
            squares.append(square)
    slab = features // (2 * n_dp)
    pieces = ((n_dp // 2, rank, slab), f32)
    document = (*wholes, *squares, own, mine, other, flag)
    clip = functools.partial(clip_kernel, 1, n_dp, n_ctx, parts)
    (send,) = in_vmem(clip, [pieces], *document)
    clip = functools.partial(clip_kernel, 0, n_dp, n_ctx, parts)
    keep, norms = in_vmem(clip, [pieces, column], *document)
    core = swap_dp(send, n_dp, 0)
    (send,) = in_vmem(core_kernel, [((rank, slab), f32)], keep, core)
    received = swap_dp(send, n_dp, 1)

    def shapes(width):
        return [((rank, width // 128 * 128 + 128), f32), ((rank, width), f32)]

    width = slab // 2
    steps = list(reversed(range(bits_of(n_ctx // 2))))
    send, keep = in_vmem(chip_kernel, shapes(width), keep, core, received, norms)
    for bit in steps[:-1]:
        width //= 2
        received = exchange(send, n_dp, n_ctx, bit, bit)
        send, keep, norms = in_vmem(step_kernel, shapes(width) + [column], keep, received, norms)
    received = exchange(send, n_dp, n_ctx, steps[-1], steps[-1])
    result, norms = pl.pallas_call(
        functools.partial(last_kernel, docs),
        out_shape=[
            jax.ShapeDtypeStruct((rank, width), f32),
            jax.ShapeDtypeStruct((1, docs), f32),
        ],
        in_specs=[vmem] * 3,
        out_specs=[vmem, vmem],
    )(*[pltpu.with_memory_space_constraint(x, pltpu.VMEM) for x in (keep, received, norms)])
    return (result.T, norms)


def on_device(out_grad, adapter_inner, doc_lengths, slab_offset, included):
    n_dp, n_ctx = lax.axis_size("dp"), lax.axis_size("ctx")
    docs = doc_lengths.shape[1]
    rows = out_grad.shape[0]
    halving = (
        n_dp == 4
        and docs == 4
        and n_ctx == 2 * docs
        and docs <= adapter_inner.shape[1]
        and 2 * (rows - 2) + (docs - 2) * LONGEST < n_ctx * rows
        and out_grad.shape[1] % (1152 * PARTS) == 0
    )
    plan = halving_plan if halving else chain_plan
    return plan(out_grad, adapter_inner, doc_lengths, slab_offset, included)


def solution(mesh):
    placed = (P(("dp", "ctx"), None), P(("dp", "ctx"), None), P("dp", None), P("dp"), P("dp", None))
    return jax.shard_map(
        on_device,
        mesh=mesh,
        in_specs=placed,
        out_specs=(P(("dp", "ctx"), None), P("dp", None)),
        check_vma=False,
    )
```
